256 devices in a mesh: row: 32 (over y, x, core), depth: 8 (over z).
Axes of the slice: x: 4, y: 4, z: 8, core: 2. Of those that a mesh axis runs over, the one named last changes fastest.
Arguments:
- density: float32 [128, 512, 1024], P('depth', 'row'), may hold values from 0.2 to 1.5
- velocity: float32 [3, 128, 512, 1024], P(None, 'depth', 'row'), may hold values from -3 to 3
- palette: float32 [3, 4], replicated, may hold values from -6 to 6
Outputs:
- filtered: float32 [4, 512, 1024], P(None, 'row', 'depth')
- settled_density: float32 [128, 512, 1024], P('depth', 'row')
- settled_velocity: float32 [3, 128, 512, 1024], P(None, 'depth', 'row')
The draws below stay inside these ranges and needn't reach their ends.
All inputs are finite; a program needn't handle non-finite values.
Results may differ from the reference program's by a relative error of at most 0.00013.
Values sent between devices are 32-bit elements; how exact they have to be, the bound alone decides.
A program may use at most 128 MiB of HBM per device.

```python
import math
import jax
import jax.numpy as jnp
from jax import lax

NX = 1024
NY = 512
NZ = 128


def level_of(rng, dims, split, smallest, high):
    def one(axis_at, shards_of):
        draws = jax.random.uniform(jax.random.fold_in(jax.random.fold_in(rng, 6), axis_at), (shards_of,), jnp.float32, smallest / len(split), high / len(split))
        return jnp.repeat(jnp.exp(draws), dims[axis_at] // shards_of).reshape((-1,) + (1,) * (len(dims) - axis_at - 1))

    factor_of = one(*split[0])
    for cut in split[1:]:
        factor_of = factor_of * one(*cut)
    return factor_of


def normal_values(key, dims, spread, bound, split=(), kind=jnp.bfloat16):
    array = spread * jax.random.normal(key, dims, jnp.float32)
    if split:
        array = array * level_of(key, dims, split, -0.22, 0.18)
    return jnp.clip(array, -bound, bound).astype(kind)


def setup_inputs(seed: int = 0) -> dict:
    arg_keys = jax.random.split(jax.random.key(seed), 4)
    density = jnp.clip(0.2 + 1.3 * jax.random.uniform(arg_keys[0], (NZ, NY, NX), jnp.float32) ** level_of(arg_keys[0], (NZ, NY, NX), ((0, 8), (1, 32)), -0.2, 0.2), 0.2, 1.5)
    velocity = normal_values(arg_keys[1], (3, NZ, NY, NX), 0.5, 3.0, ((1, 8), (2, 32)), jnp.float32)
    palette = normal_values(arg_keys[2], (3, 4), 1.5, 6.0, (), jnp.float32)
    return {"density": density, "velocity": velocity, "palette": palette}


DIFFUSION = 0.1
ADVECTION = 0.25
VISCOSITY = 0.15
FRICTION = 0.2
OPTICAL = 2.0
RANGE_SCALE = 0.1
SPACE_SCALE = 1.5


def advance(padded):
    widened = jnp.pad(padded, ((0, 0), (0, 0), (0, 0), (1, 1)))
    centre = widened[:, 1:-1, 1:-1, 1:-1]
    front_side = widened[:, :-2, 1:-1, 1:-1]
    back_side = widened[:, 2:, 1:-1, 1:-1]
    upper_side = widened[:, 1:-1, :-2, 1:-1]
    lower_side = widened[:, 1:-1, 2:, 1:-1]
    left_side = widened[:, 1:-1, 1:-1, :-2]
    right_side = widened[:, 1:-1, 1:-1, 2:]
    laplace = front_side + back_side + upper_side + lower_side + left_side + right_side - 6.0 * centre
    flux_div = 0.5 * (right_side[0] * right_side[1] - left_side[0] * left_side[1]
                      + lower_side[0] * lower_side[2] - upper_side[0] * upper_side[2]
                      + back_side[0] * back_side[3] - front_side[0] * front_side[3])
    density = centre[0]
    squared = density * density
    new_density = density + DIFFUSION * laplace[0] - ADVECTION * flux_div
    viscous = VISCOSITY * squared / (1.0 + squared)
    new_velocity = (centre[1:] + viscous * laplace[1:]) / (1.0 + FRICTION * squared)
    return jnp.concatenate([new_density[None], new_velocity], 0)


def bilateral(padded, valid):
    height = padded.shape[1] - 4
    width = padded.shape[2] - 4
    luminance = (padded[0] + padded[1] + padded[2]) / 3.0
    centre_lum = luminance[2:2 + height, 2:2 + width]
    numerator = jnp.zeros((4, height, width), jnp.float32)
    denominator = jnp.zeros((height, width), jnp.float32)
    for row_offset in range(5):
        for col_offset in range(5):
            spatial = math.exp(-((row_offset - 2) * (row_offset - 2) + (col_offset - 2) * (col_offset - 2)) / (2.0 * SPACE_SCALE * SPACE_SCALE))
            shifted = padded[:, row_offset:row_offset + height, col_offset:col_offset + width]
            shifted_lum = luminance[row_offset:row_offset + height, col_offset:col_offset + width]
            shifted_valid = valid[row_offset:row_offset + height, col_offset:col_offset + width]
            diff = shifted_lum - centre_lum
            weight = shifted_valid * spatial * jnp.exp(-diff * diff / (2.0 * RANGE_SCALE * RANGE_SCALE))
            numerator = numerator + weight[None] * shifted
            denominator = denominator + weight
    return numerator / denominator[None]


def reference(density, velocity, palette):
    volume = jnp.concatenate([density[None], velocity], 0)
    for repeat_index in range(2):
        volume = advance(jnp.pad(volume, ((0, 0), (1, 1), (1, 1), (0, 0))))
    depth_total = volume.shape[1]

    def march(running, layer):
        depth_sum, colour = running
        optical = (OPTICAL / depth_total) * layer[0] * layer[0]
        opacity = 1.0 - jnp.exp(-optical)
        shading = jax.nn.sigmoid(jnp.einsum("ck,kyx->cyx", palette, layer, precision=lax.Precision.HIGHEST))
        colour = colour + (jnp.exp(-depth_sum) * opacity)[None] * shading
        return (depth_sum + optical, colour), None

    slices = jnp.moveaxis(volume, 1, 0)
    start_sum = jnp.zeros(volume.shape[2:], jnp.float32)
    start_colour = jnp.zeros((3,) + volume.shape[2:], jnp.float32)
    (depth_sum, colour), unused_out = lax.scan(march, (start_sum, start_colour), slices)
    picture = jnp.concatenate([colour, (1.0 - jnp.exp(-depth_sum))[None]], 0)
    valid = jnp.pad(jnp.ones(picture.shape[1:], jnp.float32), 2)
    filtered = bilateral(jnp.pad(picture, ((0, 0), (2, 2), (2, 2))), valid)
    return filtered, volume[0], volume[1:]
```

```python
import functools
import math

import jax
import jax.numpy as jnp
from jax import lax
from jax.experimental import pallas as pl
from jax.experimental.pallas import tpu as pltpu
from jax.sharding import PartitionSpec as P

DIFFUSION = 0.1
ADVECTION = 0.25
VISCOSITY = 0.15
FRICTION = 0.2
OPTICAL = 2.0
RANGE_SCALE = 0.1
SPACE_SCALE = 1.5
MESH = pl.DeviceIdType.MESH
LANES = 128
SUB = 8


def shifted_pair(before, here, after, first, last):
    left = pltpu.roll(jnp.where(last, before, here), 1, 1)
    right = pltpu.roll(jnp.where(first, after, here), LANES - 1, 1)
    return left, right


def step_tile(ref, z, block, row, first, last):
    def get(k, dz=0, dy=0, dx=0):
        return ref[k, z + dz, block + dx, pl.ds(row + dy, SUB), :]

    here = [get(k) for k in range(4)]
    sides = [
        shifted_pair(get(k, dx=-1), here[k], get(k, dx=1), first, last) for k in range(4)
    ]
    up = [get(k, dy=-1) for k in range(4)]
    down = [get(k, dy=1) for k in range(4)]
    front = [get(k, dz=-1) for k in range(4)]
    back = [get(k, dz=1) for k in range(4)]
    left = [s[0] for s in sides]
    right = [s[1] for s in sides]
    sums = [
        (left[k] + right[k]) + (up[k] + down[k]) + (front[k] + back[k]) for k in range(4)
    ]
    flux = (
        (right[0] * right[1] - left[0] * left[1])
        + (down[0] * down[2] - up[0] * up[2])
        + (back[0] * back[3] - front[0] * front[3])
    )
    r = here[0]
    squared = r * r
    new_r = (1.0 - 6.0 * DIFFUSION) * r + DIFFUSION * sums[0] - (0.5 * ADVECTION) * flux
    one = 1.0 + squared
    drag = 1.0 + FRICTION * squared
    inverse = 1.0 / (one * drag)
    side_w = VISCOSITY * squared * inverse
    own_w = one * inverse - 6.0 * side_w
    return [new_r] + [own_w * here[k] + side_w * sums[k] for k in range(1, 4)]


def kernel(
    depth_count,
    row_count,
    dens,
    vel,
    pal,
    filtered,
    out_d,
    out_v,
    q0,
    q1,
    corner_d,
    corner_v,
    piece,
    pieces,
    ext,
    load_sem,
    zsend,
    zrecv,
    rsend,
    rrecv,
    csend,
    crecv,
    psend,
    precv,
    hsend,
    hrecv,
):
    zn, yn = dens.shape[0], dens.shape[1]
    chunks = dens.shape[2] // LANES
    tiles = yn // SUB
    d = lax.axis_index("depth")
    r = lax.axis_index("row")
    has = {-1: (d > 0, r > 0), 1: (d < depth_count - 1, r < row_count - 1)}

    def present(dd, dr):
        ok = None
        for step, which in ((dd, 0), (dr, 1)):
            if step:
                ok = has[step][which] if ok is None else ok & has[step][which]
        return ok

    def where_is(dd, dr):
        return {"depth": d + dd, "row": r + dr}

    around = [(dd, dr) for dd in (-1, 0, 1) for dr in (-1, 0, 1) if dd or dr]
    diagonal = [(dd, dr) for dd in (-1, 1) for dr in (-1, 1)]

    barrier = pltpu.get_barrier_semaphore()
    count = jnp.int32(depth_count - 1)
    for dd, dr in around:
        if dr == 0:
            continue
        ok = present(dd, dr)
        count = count + ok.astype(jnp.int32)

        @pl.when(ok)
        def _(dd=dd, dr=dr):
            pl.semaphore_signal(barrier, inc=1, device_id=where_is(dd, dr), device_id_type=MESH)

    for k in range(1, depth_count):
        other = lax.rem(d + k, depth_count)
        pl.semaphore_signal(
            barrier, inc=1, device_id={"depth": other, "row": r}, device_id_type=MESH
        )

    def cols(c):
        return pl.ds(pl.multiple_of(c * LANES, LANES), LANES)

    def loads(c):
        rows = pl.ds(SUB, yn)
        return (
            pltpu.make_async_copy(
                dens.at[:, :, cols(c)], q0.at[0, pl.ds(2, zn), 1 + c, rows, :], load_sem.at[0, c]
            ),
            pltpu.make_async_copy(
                vel.at[:, :, :, cols(c)],
                q0.at[pl.ds(1, 3), pl.ds(2, zn), 1 + c, rows, :],
                load_sem.at[1, c],
            ),
        )

    def zcopies(c, dd):
        src = pl.ds(0, 2) if dd < 0 else pl.ds(zn - 2, 2)
        dst = pl.ds(zn + 2, 2) if dd < 0 else pl.ds(0, 2)
        side = (dd + 1) // 2
        rows = pl.ds(SUB, yn)
        return (
            pltpu.make_async_remote_copy(
                dens.at[src, :, cols(c)],
                q0.at[0, dst, 1 + c, rows, :],
                zsend.at[side, 0, c],
                zrecv.at[side, 0, c],
                device_id=where_is(dd, 0),
                device_id_type=MESH,
            ),
            pltpu.make_async_remote_copy(
                vel.at[:, src, :, cols(c)],
                q0.at[pl.ds(1, 3), dst, 1 + c, rows, :],
                zsend.at[side, 1, c],
                zrecv.at[side, 1, c],
                device_id=where_is(dd, 0),
                device_id_type=MESH,
            ),
        )

    def rcopies(c, dr):
        src = pl.ds(0, 2) if dr < 0 else pl.ds(yn - 2, 2)
        dst = pl.ds(SUB + yn, 2) if dr < 0 else pl.ds(SUB - 2, 2)
        side = (dr + 1) // 2
        return (
            pltpu.make_async_remote_copy(
                dens.at[:, src, cols(c)],
                q0.at[0, pl.ds(2, zn), 1 + c, dst, :],
                rsend.at[side, 0, c],
                rrecv.at[side, 0, c],
                device_id=where_is(0, dr),
                device_id_type=MESH,
            ),
            pltpu.make_async_remote_copy(
                vel.at[:, :, src, cols(c)],
                q0.at[pl.ds(1, 3), pl.ds(2, zn), 1 + c, dst, :],
                rsend.at[side, 1, c],
                rrecv.at[side, 1, c],
                device_id=where_is(0, dr),
                device_id_type=MESH,
            ),
        )

    def ccopies(dd, dr):
        z = pl.ds(0, 1) if dd < 0 else pl.ds(zn - 1, 1)
        y = pl.ds(0, 1) if dr < 0 else pl.ds(yn - 1, 1)
        slot = diagonal.index((-dd, -dr))
        return (
            pltpu.make_async_remote_copy(
                dens.at[z, y, :],
                corner_d.at[slot],
                csend.at[0, slot],
                crecv.at[0, slot],
                device_id=where_is(dd, dr),
                device_id_type=MESH,
            ),
            pltpu.make_async_remote_copy(
                vel.at[:, z, y, :],
                corner_v.at[slot],
                csend.at[1, slot],
                crecv.at[1, slot],
                device_id=where_is(dd, dr),
                device_id_type=MESH,
            ),
        )

    def start_loads(c, carry):
        for copy in loads(c):
            copy.start()
        return carry

    lax.fori_loop(0, chunks, start_loads, 0)
    pl.semaphore_wait(barrier, count)

    def start_chunk(c, carry):
        for dd in (-1, 1):

            @pl.when(has[dd][0])
            def _(dd=dd):
                for copy in zcopies(c, dd):
                    copy.start()

        for dr in (-1, 1):

            @pl.when(has[dr][1])
            def _(dr=dr):
                for copy in rcopies(c, dr):
                    copy.start()

        return carry

    for dd, dr in diagonal:

        @pl.when(present(dd, dr))
        def _(dd=dd, dr=dr):
            for copy in ccopies(dd, dr):
                copy.start()

    lax.fori_loop(0, chunks, start_chunk, 0)

    zero = jnp.zeros((SUB, LANES), jnp.float32)

    def pad_q0(z, carry):
        for k in range(4):
            for block in (0, chunks + 1):
                for t in range(tiles + 2):
                    q0[k, z, block, pl.ds(t * SUB, SUB), :] = zero
        return carry

    def pad_q1(z, carry):
        for k in range(4):
            for block in (0, chunks + 1):
                for t in range(tiles + 1):
                    q1[k, z, block, pl.ds(t * SUB, SUB), :] = zero
        return carry

    lax.fori_loop(1, zn + 3, pad_q0, 0)
    lax.fori_loop(0, zn + 2, pad_q1, 0)
    for dd in (-1, 1):
        layer = 1 if dd < 0 else zn + 2

        @pl.when(jnp.logical_not(has[dd][0]))
        def _(layer=layer):
            def clear(c, carry):
                for k in range(4):
                    for t in range(tiles + 2):
                        q0[k, layer, 1 + c, pl.ds(t * SUB, SUB), :] = zero
                return carry

            lax.fori_loop(0, chunks, clear, 0)

    for dr in (-1, 1):
        top = 0 if dr < 0 else SUB + yn

        @pl.when(jnp.logical_not(has[dr][1]))
        def _(top=top):
            def clear(z, carry):
                for k in range(4):
                    for c in range(chunks):
                        q0[k, z, 1 + c, pl.ds(top, SUB), :] = zero
                return carry

            lax.fori_loop(1, zn + 3, clear, 0)

    lane = lax.broadcasted_iota(jnp.int32, (SUB, LANES), 1)
    sublane = lax.broadcasted_iota(jnp.int32, (SUB, LANES), 0)
    first, last = lane == 0, lane == LANES - 1

    for dd, dr in diagonal:

        @pl.when(present(dd, dr))
        def _(dd=dd, dr=dr):
            slot = diagonal.index((dd, dr))
            for copy in ccopies(-dd, -dr):
                copy.wait_recv()
            z = 1 if dd < 0 else zn + 2
            y = SUB - 1 if dr < 0 else SUB + yn
            for c in range(chunks):
                at = pl.ds(c * LANES, LANES)
                q0[0, z, 1 + c, pl.ds(y, 1), :] = corner_d[slot, 0, :, at]
                for k in range(3):
                    q0[1 + k, z, 1 + c, pl.ds(y, 1), :] = corner_v[slot, k, 0, :, at]

    def wait_chunk(c):
        for copy in loads(c):
            copy.wait()
        for dd in (-1, 1):

            @pl.when(has[dd][0])
            def _(dd=dd):
                for copy in zcopies(c, -dd):
                    copy.wait_recv()

        for dr in (-1, 1):

            @pl.when(has[dr][1])
            def _(dr=dr):
                for copy in rcopies(c, -dr):
                    copy.wait_recv()

    low_row = jnp.where(r > 0, -1, 0)
    high_row = jnp.where(r < row_count - 1, yn, yn - 1)
    row_ok = []
    for t in range(tiles + 1):
        y = sublane + (t * SUB - 1)
        row_ok.append((y >= low_row) & (y <= high_row))
    low_z = jnp.where(d > 0, 0, 1)
    high_z = jnp.where(d < depth_count - 1, zn + 1, zn)

    def step_one(c):
        def layer(z, carry):
            inside = (z >= low_z) & (z <= high_z)
            for t in range(tiles + 1):
                new = step_tile(q0, z + 1, 1 + c, SUB - 1 + t * SUB, first, last)
                ok = row_ok[t] & inside
                for k in range(4):
                    q1[k, z, 1 + c, pl.ds(t * SUB, SUB), :] = jnp.where(ok, new[k], 0.0)
            return carry

        lax.fori_loop(0, zn + 2, layer, 0)

    weights = [[0.5 * pal[i, k] for k in range(4)] for i in range(3)]
    thickness = OPTICAL / (zn * depth_count)

    def step_two(c):
        at = cols(c)

        def layer(z, carry):
            out = []
            for t in range(tiles):
                through, *shades = carry[t]
                new = step_tile(q1, z + 1, 1 + c, 1 + t * SUB, first, last)
                rows = pl.ds(t * SUB, SUB)
                out_d[z, rows, at] = new[0]
                for k in range(3):
                    out_v[k, z, rows, at] = new[1 + k]
                beyond = through * jnp.exp((-thickness) * new[0] * new[0])
                emitted = through - beyond
                lit = []
                for i in range(3):
                    dot = weights[i][0] * new[0]
                    for k in range(1, 4):
                        dot = dot + weights[i][k] * new[k]
                    lit.append(shades[i] + emitted * jnp.tanh(dot))
                out.append((beyond, *lit))
            return tuple(out)

        one = jnp.ones((SUB, LANES), jnp.float32)
        start = tuple((one, zero, zero, zero) for _ in range(tiles))
        done = lax.fori_loop(0, zn, layer, start)
        for t in range(tiles):
            through, *shades = done[t]
            rows = pl.ds(t * SUB, SUB)
            for i in range(3):
                piece[c, i, rows, :] = 0.5 * ((1.0 - through) + shades[i])
            piece[c, 3, rows, :] = through

    def pcopy(c, source):
        return pltpu.make_async_remote_copy(
            piece.at[c],
            pieces.at[source],
            psend.at[c],
            precv.at[source],
            device_id={"depth": c, "row": r},
            device_id_type=MESH,
        )

    wait_chunk(0)

    def work(i, carry):
        @pl.when(i + 1 < chunks)
        def _():
            wait_chunk(i + 1)

        @pl.when(i < chunks)
        def _():
            step_one(i)

        @pl.when(i >= 1)
        def _():
            c = i - 1
            step_two(c)

            @pl.when(c != d)
            def _():
                pcopy(c, d).start()

            @pl.when(c == d)
            def _():
                pieces[d] = piece[c]

        return carry

    lax.fori_loop(0, chunks + 1, work, 0)

    def wait_piece(k, carry):
        @pl.when(k != d)
        def _():
            pcopy(k, k).wait_recv()

        return carry

    lax.fori_loop(0, depth_count, wait_piece, 0)

    for t in range(tiles):
        rows = pl.ds(t * SUB, SUB)
        through = pieces[0, 3, rows, :]
        colour = [pieces[0, i, rows, :] for i in range(3)]
        for k in range(1, depth_count):
            for i in range(3):
                colour[i] = colour[i] + through * pieces[k, i, rows, :]
            through = through * pieces[k, 3, rows, :]
        for i in range(3):
            ext[1, i, pl.ds(SUB + t * SUB, SUB), :] = colour[i]
        ext[1, 3, pl.ds(SUB + t * SUB, SUB), :] = 1.0 - through

    def hcopy(dd, dr):
        if dr == 0:
            src = dst = pl.ds(SUB, yn)
        elif dr < 0:
            src, dst = pl.ds(SUB, SUB), pl.ds(SUB + yn, SUB)
        else:
            src, dst = pl.ds(yn, SUB), pl.ds(0, SUB)
        slot = around.index((-dd, -dr))
        return pltpu.make_async_remote_copy(
            ext.at[1, :, src, :],
            ext.at[1 - dd, :, dst, :],
            hsend.at[slot],
            hrecv.at[slot],
            device_id=where_is(dd, dr),
            device_id_type=MESH,
        )

    for dd, dr in around:

        @pl.when(present(dd, dr))
        def _(dd=dd, dr=dr):
            hcopy(dd, dr).start()

    for dd, dr in around:

        @pl.when(present(dd, dr))
        def _(dd=dd, dr=dr):
            hcopy(-dd, -dr).wait_recv()

    for t in range(tiles):
        own = [ext[1, i, pl.ds(SUB + t * SUB, SUB), :] for i in range(4)]
        centre = (own[0] + own[1] + own[2]) * (1.0 / 3.0)
        top = [zero] * 4
        bottom = zero
        for dy in range(-2, 3):
            rows = pl.ds(SUB + t * SUB + dy, SUB)
            y = sublane + (r * yn + t * SUB + dy)
            y_ok = (y >= 0) & (y < yn * row_count)
            mid = [ext[1, i, rows, :] for i in range(4)]
            before = [ext[0, i, rows, :] for i in range(4)]
            after = [ext[2, i, rows, :] for i in range(4)]
            for dx in range(-2, 3):
                x = lane + (d * LANES + dx)
                ok = y_ok & (x >= 0) & (x < LANES * depth_count)
                if dx < 0:
                    pixel = [
                        pltpu.roll(jnp.where(lane >= LANES + dx, before[i], mid[i]), -dx, 1)
                        for i in range(4)
                    ]
                elif dx > 0:
                    pixel = [
                        pltpu.roll(jnp.where(lane < dx, after[i], mid[i]), LANES - dx, 1)
                        for i in range(4)
                    ]
                else:
                    pixel = mid
                pixel = [jnp.where(ok, p, 0.0) for p in pixel]
                space = math.exp(-(dx * dx + dy * dy) / (2.0 * SPACE_SCALE * SPACE_SCALE))
                diff = (pixel[0] + pixel[1] + pixel[2]) * (1.0 / 3.0) - centre
                close = jnp.exp(diff * diff * (-1.0 / (2.0 * RANGE_SCALE * RANGE_SCALE)))
                weight = jnp.where(ok, space * close, 0.0)
                top = [top[i] + weight * pixel[i] for i in range(4)]
                bottom = bottom + weight
        for i in range(4):
            filtered[i, pl.ds(t * SUB, SUB), :] = top[i] / bottom

    def sent(c, carry):
        for dd in (-1, 1):

            @pl.when(has[dd][0])
            def _(dd=dd):
                for copy in zcopies(c, dd):
                    copy.wait_send()

        for dr in (-1, 1):

            @pl.when(has[dr][1])
            def _(dr=dr):
                for copy in rcopies(c, dr):
                    copy.wait_send()

        @pl.when(c != d)
        def _():
            pcopy(c, d).wait_send()

        return carry

    lax.fori_loop(0, chunks, sent, 0)
    for dd, dr in diagonal:

        @pl.when(present(dd, dr))
        def _(dd=dd, dr=dr):
            for copy in ccopies(dd, dr):
                copy.wait_send()

    for dd, dr in around:

        @pl.when(present(dd, dr))
        def _(dd=dd, dr=dr):
            hcopy(dd, dr).wait_send()


def body(depth_count, row_count, density, velocity, palette):
    zn, yn, xn = density.shape
    chunks = xn // LANES
    assert chunks == depth_count and yn % SUB == 0
    f32 = jnp.float32
    dma = pltpu.SemaphoreType.DMA
    vmem = pltpu.VMEM
    return pl.pallas_call(
        functools.partial(kernel, depth_count, row_count),
        out_shape=(
            jax.ShapeDtypeStruct((4, yn, LANES), f32),
            jax.ShapeDtypeStruct(density.shape, f32),
            jax.ShapeDtypeStruct(velocity.shape, f32),
        ),
        in_specs=[
            pl.BlockSpec(memory_space=pl.ANY),
            pl.BlockSpec(memory_space=pl.ANY),
            pl.BlockSpec(memory_space=pltpu.SMEM),
        ],
        out_specs=(pl.BlockSpec(memory_space=vmem),) * 3,
        scratch_shapes=[
            vmem((4, zn + 4, chunks + 2, yn + 2 * SUB, LANES), f32),
            vmem((4, zn + 2, chunks + 2, yn + SUB, LANES), f32),
            vmem((4, 1, 1, xn), f32),
            vmem((4, 3, 1, 1, xn), f32),
            vmem((chunks, 4, yn, LANES), f32),
            vmem((depth_count, 4, yn, LANES), f32),
            vmem((3, 4, yn + 2 * SUB, LANES), f32),
            dma((2, chunks)),
            dma((2, 2, chunks)),
            dma((2, 2, chunks)),
            dma((2, 2, chunks)),
            dma((2, 2, chunks)),
            dma((2, 4)),
            dma((2, 4)),
            dma((chunks,)),
            dma((depth_count,)),
            dma((8,)),
            dma((8,)),
        ],
        compiler_params=pltpu.CompilerParams(
            collective_id=0, has_side_effects=True, vmem_limit_bytes=48 * 2**20
        ),
        name="rheology",
    )(density, velocity, palette)


def solution(mesh):
    in_specs = (P("depth", "row", None), P(None, "depth", "row", None), P())
    out_specs = (P(None, "row", "depth"), P("depth", "row", None), P(None, "depth", "row", None))
    run = functools.partial(body, mesh.shape["depth"], mesh.shape["row"])
    return jax.shard_map(run, mesh=mesh, in_specs=in_specs, out_specs=out_specs, check_vma=False)
```

```python
import functools
import math

import jax
import jax.numpy as jnp
from jax import lax
from jax.experimental import pallas as pl
from jax.experimental.pallas import tpu as pltpu
from jax.sharding import PartitionSpec as P

DIFFUSION = 0.1
ADVECTION = 0.25
VISCOSITY = 0.15
FRICTION = 0.2
OPTICAL = 2.0
RANGE_SCALE = 0.1
SPACE_SCALE = 1.5
MESH = pl.DeviceIdType.MESH
LANES = 128
SUB = 8
PARTS = 2


def shifted_pair(before, here, after, first, last):
    left = pltpu.roll(jnp.where(last, before, here), 1, 1)
    right = pltpu.roll(jnp.where(first, after, here), LANES - 1, 1)
    return left, right


def divisor(n, most):
    return max([k for k in range(1, most + 1) if n and n % k == 0], default=1)


def step_tile(ref, z, block, row, first, last):
    def get(k, dz=0, dy=0, dx=0):
        return ref[k, z + dz, block + dx, pl.ds(row + dy, SUB), :]

    here = [get(k) for k in range(4)]
    sides = [
        shifted_pair(get(k, dx=-1), here[k], get(k, dx=1), first, last) for k in range(4)
    ]
    up = [get(k, dy=-1) for k in range(4)]
    down = [get(k, dy=1) for k in range(4)]
    front = [get(k, dz=-1) for k in range(4)]
    back = [get(k, dz=1) for k in range(4)]
    left = [s[0] for s in sides]
    right = [s[1] for s in sides]
    sums = [
        (left[k] + right[k]) + (up[k] + down[k]) + (front[k] + back[k]) for k in range(4)
    ]
    flux = (
        (right[0] * right[1] - left[0] * left[1])
        + (down[0] * down[2] - up[0] * up[2])
        + (back[0] * back[3] - front[0] * front[3])
    )
    r = here[0]
    squared = r * r
    new_r = (1.0 - 6.0 * DIFFUSION) * r + DIFFUSION * sums[0] - (0.5 * ADVECTION) * flux
    one = 1.0 + squared
    drag = 1.0 + FRICTION * squared
    inverse = 1.0 / (one * drag)
    side_w = VISCOSITY * squared * inverse
    own_w = one * inverse - 6.0 * side_w
    return [new_r] + [own_w * here[k] + side_w * sums[k] for k in range(1, 4)]


def kernel(
    depth_count,
    row_count,
    dens,
    vel,
    pal_hbm,
    mid,
    side,
    out_d,
    out_v,
    q0,
    q1,
    corner_d,
    corner_v,
    middle,
    piece,
    pieces,
    edge,
    pal,
    load_sem,
    pal_sem,
    zsend,
    zrecv,
    rsend,
    rrecv,
    csend,
    crecv,
    psend,
    precv,
    hsend,
    hrecv,
):
    zn, yn = dens.shape[0], dens.shape[1]
    chunks = dens.shape[2] // LANES
    tiles = yn // SUB
    d = lax.axis_index("depth")
    r = lax.axis_index("row")
    has = {-1: (d > 0, r > 0), 1: (d < depth_count - 1, r < row_count - 1)}

    def present(dd, dr):
        ok = None
        for step, which in ((dd, 0), (dr, 1)):
            if step:
                ok = has[step][which] if ok is None else ok & has[step][which]
        return ok

    def where_is(dd, dr):
        return {"depth": d + dd, "row": r + dr}

    around = [(dd, dr) for dd in (-1, 0, 1) for dr in (-1, 0, 1) if dd or dr]
    diagonal = [(dd, dr) for dd in (-1, 1) for dr in (-1, 1)]

    barrier = pltpu.get_barrier_semaphore()
    count = jnp.int32(depth_count - 1)
    for dd, dr in around:
        if dr == 0:
            continue
        ok = present(dd, dr)
        count = count + ok.astype(jnp.int32)

        @pl.when(ok)
        def _(dd=dd, dr=dr):
            pl.semaphore_signal(barrier, inc=1, device_id=where_is(dd, dr), device_id_type=MESH)

    for k in range(1, depth_count):
        other = lax.rem(d + k, depth_count)
        pl.semaphore_signal(
            barrier, inc=1, device_id={"depth": other, "row": r}, device_id_type=MESH
        )

    def cols(c):
        return pl.ds(pl.multiple_of(c * LANES, LANES), LANES)

    def loads(c):
        rows = pl.ds(SUB, yn)
        return (
            pltpu.make_async_copy(
                dens.at[:, :, cols(c)], q0.at[0, pl.ds(2, zn), 1 + c, rows, :], load_sem.at[0, c]
            ),
            pltpu.make_async_copy(
                vel.at[:, :, :, cols(c)],
                q0.at[pl.ds(1, 3), pl.ds(2, zn), 1 + c, rows, :],
                load_sem.at[1, c],
            ),
        )

    def zcopies(c, dd):
        src = pl.ds(0, 2) if dd < 0 else pl.ds(zn - 2, 2)
        dst = pl.ds(zn + 2, 2) if dd < 0 else pl.ds(0, 2)
        side = (dd + 1) // 2
        rows = pl.ds(SUB, yn)
        return (
            pltpu.make_async_remote_copy(
                dens.at[src, :, cols(c)],
                q0.at[0, dst, 1 + c, rows, :],
                zsend.at[side, 0, c],
                zrecv.at[side, 0, c],
                device_id=where_is(dd, 0),
                device_id_type=MESH,
            ),
            pltpu.make_async_remote_copy(
                vel.at[:, src, :, cols(c)],
                q0.at[pl.ds(1, 3), dst, 1 + c, rows, :],
                zsend.at[side, 1, c],
                zrecv.at[side, 1, c],
                device_id=where_is(dd, 0),
                device_id_type=MESH,
            ),
        )

    def rcopies(c, dr):
        src = pl.ds(0, 2) if dr < 0 else pl.ds(yn - 2, 2)
        dst = pl.ds(SUB + yn, 2) if dr < 0 else pl.ds(SUB - 2, 2)
        side = (dr + 1) // 2
        return (
            pltpu.make_async_remote_copy(
                dens.at[:, src, cols(c)],
                q0.at[0, pl.ds(2, zn), 1 + c, dst, :],
                rsend.at[side, 0, c],
                rrecv.at[side, 0, c],
                device_id=where_is(0, dr),
                device_id_type=MESH,
            ),
            pltpu.make_async_remote_copy(
                vel.at[:, :, src, cols(c)],
                q0.at[pl.ds(1, 3), pl.ds(2, zn), 1 + c, dst, :],
                rsend.at[side, 1, c],
                rrecv.at[side, 1, c],
                device_id=where_is(0, dr),
                device_id_type=MESH,
            ),
        )

    def ccopies(dd, dr):
        z = pl.ds(0, 1) if dd < 0 else pl.ds(zn - 1, 1)
        y = pl.ds(0, 1) if dr < 0 else pl.ds(yn - 1, 1)
        slot = diagonal.index((-dd, -dr))
        return (
            pltpu.make_async_remote_copy(
                dens.at[z, y, :],
                corner_d.at[slot],
                csend.at[0, slot],
                crecv.at[0, slot],
                device_id=where_is(dd, dr),
                device_id_type=MESH,
            ),
            pltpu.make_async_remote_copy(
                vel.at[:, z, y, :],
                corner_v.at[slot],
                csend.at[1, slot],
                crecv.at[1, slot],
                device_id=where_is(dd, dr),
                device_id_type=MESH,
            ),
        )

    def start_loads(c, carry):
        for copy in loads(c):
            copy.start()
        return carry

    lax.fori_loop(0, chunks, start_loads, 0)
    pal_copy = pltpu.make_async_copy(pal_hbm, pal, pal_sem)
    pal_copy.start()
    pl.semaphore_wait(barrier, count)

    def start_layers(c, carry):
        for dd in (-1, 1):

            @pl.when(has[dd][0])
            def _(dd=dd):
                for copy in zcopies(c, dd):
                    copy.start()

        return carry

    def start_rows(c, carry):
        for dr in (-1, 1):

            @pl.when(has[dr][1])
            def _(dr=dr):
                for copy in rcopies(c, dr):
                    copy.start()

        return carry

    for dd, dr in diagonal:

        @pl.when(present(dd, dr))
        def _(dd=dd, dr=dr):
            for copy in ccopies(dd, dr):
                copy.start()

    start_layers(0, 0)
    lax.fori_loop(0, chunks, start_rows, 0)
    lax.fori_loop(1, chunks, start_layers, 0)

    zero = jnp.zeros((SUB, LANES), jnp.float32)

    def pad_q0(z, carry):
        for k in range(4):
            for block in (0, chunks + 1):
                for t in range(tiles + 2):
                    q0[k, z, block, pl.ds(t * SUB, SUB), :] = zero
        return carry

    def pad_q1(z, carry):
        for k in range(4):
            for block in (0, chunks + 1):
                for t in range(tiles + 1):
                    q1[k, z, block, pl.ds(t * SUB, SUB), :] = zero
        return carry

    lax.fori_loop(1, zn + 3, pad_q0, 0)
    lax.fori_loop(0, zn + 2, pad_q1, 0)
    for dd in (-1, 1):
        layer = 1 if dd < 0 else zn + 2

        @pl.when(jnp.logical_not(has[dd][0]))
        def _(layer=layer):
            def clear(c, carry):
                for k in range(4):
                    for t in range(tiles + 2):
                        q0[k, layer, 1 + c, pl.ds(t * SUB, SUB), :] = zero
                return carry

            lax.fori_loop(0, chunks, clear, 0)

    for dr in (-1, 1):
        top = 0 if dr < 0 else SUB + yn

        @pl.when(jnp.logical_not(has[dr][1]))
        def _(top=top):
            def clear(z, carry):
                for k in range(4):
                    for c in range(chunks):
                        q0[k, z, 1 + c, pl.ds(top, SUB), :] = zero
                return carry

            lax.fori_loop(1, zn + 3, clear, 0)

    lane = lax.broadcasted_iota(jnp.int32, (SUB, LANES), 1)
    sublane = lax.broadcasted_iota(jnp.int32, (SUB, LANES), 0)
    first, last = lane == 0, lane == LANES - 1

    def wait_layers(c):
        for dd in (-1, 1):

            @pl.when(has[dd][0])
            def _(dd=dd):
                for copy in zcopies(c, -dd):
                    copy.wait_recv()

    def wait_own(c):
        for copy in loads(c):
            copy.wait()

    def wait_rows(c):
        for dr in (-1, 1):

            @pl.when(has[dr][1])
            def _(dr=dr):
                for copy in rcopies(c, -dr):
                    copy.wait_recv()

    low_row = jnp.where(r > 0, -1, 0)
    high_row = jnp.where(r < row_count - 1, yn, yn - 1)
    row_ok = []
    for t in range(tiles + 1):
        y = sublane + (t * SUB - 1)
        row_ok.append((y >= low_row) & (y <= high_row))
    low_z = jnp.where(d > 0, 0, 1)
    high_z = jnp.where(d < depth_count - 1, zn + 1, zn)

    def first_step(c, z, which, edge_layer):
        inside = (z >= low_z) & (z <= high_z) if edge_layer else None
        for t in which:
            new = step_tile(q0, z + 1, 1 + c, SUB - 1 + t * SUB, first, last)
            ok = row_ok[t] if t in (0, tiles) else None
            if edge_layer:
                ok = inside if ok is None else ok & inside
            for k in range(4):
                q1[k, z, 1 + c, pl.ds(t * SUB, SUB), :] = (
                    new[k] if ok is None else jnp.where(ok, new[k], 0.0)
                )

    def first_inner(c, which):
        def layer(z, carry):
            first_step(c, z, which, False)
            return carry

        lax.fori_loop(2, zn, layer, 0, unroll=divisor(zn - 2, 7))

    def first_outer(c):
        for z in (0, 1, zn, zn + 1):
            first_step(c, z, range(tiles + 1), z in (0, zn + 1))

    pal_copy.wait()
    weights = [[0.5 * pal[i, k] for k in range(4)] for i in range(3)]
    thickness = OPTICAL / (zn * depth_count)

    def second_step(c, z, carry):
        at = cols(c)
        out = []
        for t in range(tiles):
            through, *shades = carry[t]
            new = step_tile(q1, z + 1, 1 + c, 1 + t * SUB, first, last)
            rows = pl.ds(t * SUB, SUB)
            out_d[z, rows, at] = new[0]
            for k in range(3):
                out_v[k, z, rows, at] = new[1 + k]
            beyond = through * jnp.exp((-thickness) * new[0] * new[0])
            emitted = through - beyond
            lit = []
            for i in range(3):
                dot = weights[i][0] * new[0]
                for k in range(1, 4):
                    dot = dot + weights[i][k] * new[k]
                lit.append(shades[i] + emitted * jnp.tanh(dot))
            out.append((beyond, *lit))
        return tuple(out)

    clear_view = tuple((jnp.ones((SUB, LANES), jnp.float32), zero, zero, zero) for _ in range(tiles))

    def second_inner(c):
        def layer(z, carry):
            return second_step(c, z, carry)

        done = lax.fori_loop(2, zn - 2, layer, clear_view, unroll=divisor(zn - 4, 6))
        for t in range(tiles):
            for i in range(4):
                middle[c, i, pl.ds(t * SUB, SUB), :] = done[t][i]

    def second_outer(c):
        view = clear_view
        for z in (0, 1):
            view = second_step(c, z, view)
        joined = []
        for t in range(tiles):
            through, *shades = view[t]
            own = [middle[c, i, pl.ds(t * SUB, SUB), :] for i in range(4)]
            joined.append(
                (through * own[0], *(shades[i] + through * own[1 + i] for i in range(3)))
            )
        view = tuple(joined)
        for z in (zn - 2, zn - 1):
            view = second_step(c, z, view)
        for t in range(tiles):
            through, *shades = view[t]
            rows = pl.ds(t * SUB, SUB)
            for i in range(3):
                piece[c, i, rows, :] = 0.5 * ((1.0 - through) + shades[i])
            piece[c, 3, rows, :] = through

    def pcopy(c, source):
        return pltpu.make_async_remote_copy(
            piece.at[c],
            pieces.at[source],
            psend.at[c],
            precv.at[source],
            device_id={"depth": c, "row": r},
            device_id_type=MESH,
        )

    def hand_over(c):
        @pl.when(c != d)
        def _():
            pcopy(c, d).start()

        @pl.when(c == d)
        def _():
            pieces[d] = piece[c]

    wait_own(0)

    def innermost(i, carry):
        @pl.when(i + 1 < chunks)
        def _():
            wait_own(i + 1)

        first_inner(i, range(1, tiles))
        return carry

    lax.fori_loop(0, chunks, innermost, 0)
    wait_rows(0)

    def inner(i, carry):
        @pl.when(i + 1 < chunks)
        def _():
            wait_rows(i + 1)

        @pl.when(i < chunks)
        def _():
            first_inner(i, (0, tiles))

        @pl.when(i >= 1)
        def _():
            second_inner(i - 1)

        return carry

    lax.fori_loop(0, chunks + 1, inner, 0)

    for dd, dr in diagonal:

        @pl.when(present(dd, dr))
        def _(dd=dd, dr=dr):
            slot = diagonal.index((dd, dr))
            for copy in ccopies(-dd, -dr):
                copy.wait_recv()
            z = 1 if dd < 0 else zn + 2
            y = SUB - 1 if dr < 0 else SUB + yn
            for c in range(chunks):
                at = pl.ds(c * LANES, LANES)
                q0[0, z, 1 + c, pl.ds(y, 1), :] = corner_d[slot, 0, :, at]
                for k in range(3):
                    q0[1 + k, z, 1 + c, pl.ds(y, 1), :] = corner_v[slot, k, 0, :, at]

    wait_layers(0)

    def outer(i, carry):
        @pl.when(i + 1 < chunks)
        def _():
            wait_layers(i + 1)

        @pl.when(i < chunks)
        def _():
            first_outer(i)

        @pl.when(i >= 1)
        def _():
            second_outer(i - 1)
            hand_over(i - 1)

        return carry

    lax.fori_loop(0, chunks + 1, outer, 0)

    def sent(c, carry):
        for dd in (-1, 1):

            @pl.when(has[dd][0])
            def _(dd=dd):
                for copy in zcopies(c, dd):
                    copy.wait_send()

        for dr in (-1, 1):

            @pl.when(has[dr][1])
            def _(dr=dr):
                for copy in rcopies(c, dr):
                    copy.wait_send()

        return carry

    lax.fori_loop(0, chunks, sent, 0)
    for dd, dr in diagonal:

        @pl.when(present(dd, dr))
        def _(dd=dd, dr=dr):
            for copy in ccopies(dd, dr):
                copy.wait_send()

    def wait_piece(k, carry):
        @pl.when(k != d)
        def _():
            pcopy(k, k).wait_recv()

        return carry

    lax.fori_loop(0, depth_count, wait_piece, 0)

    for t in range(tiles):
        rows = pl.ds(t * SUB, SUB)
        through = pieces[0, 3, rows, :]
        colour = [pieces[0, i, rows, :] for i in range(3)]
        for k in range(1, depth_count):
            for i in range(3):
                colour[i] = colour[i] + through * pieces[k, i, rows, :]
            through = through * pieces[k, 3, rows, :]
        pixel = colour + [1.0 - through]
        rows = pl.ds(SUB + t * SUB, SUB)
        left, right = pixel[0], pltpu.roll(pixel[0], 2, 1)
        for i in range(4):
            mid[i, rows, :] = pixel[i]
            if i:
                left = jnp.where(lane >= 2 * i, pltpu.roll(pixel[i], 2 * i, 1), left)
                right = jnp.where(lane >= 2 * i, pltpu.roll(pixel[i], 2 * i + 2, 1), right)
        edge[0, rows, :] = left
        edge[1, rows, :] = right

    def hcopy(dd, dr):
        if dr == 0:
            src = dst = pl.ds(SUB, yn)
        elif dr < 0:
            src, dst = pl.ds(SUB, 2), pl.ds(SUB + yn, 2)
        else:
            src, dst = pl.ds(SUB + yn - 2, 2), pl.ds(SUB - 2, 2)
        slot = around.index((-dd, -dr))
        if dd:
            ends = edge.at[(dd + 1) // 2, src, :], side.at[(1 - dd) // 2, dst, :]
        else:
            ends = mid.at[:, src, :], mid.at[:, dst, :]
        return pltpu.make_async_remote_copy(
            *ends,
            hsend.at[slot],
            hrecv.at[slot],
            device_id=where_is(dd, dr),
            device_id_type=MESH,
        )

    for dd, dr in around:

        @pl.when(present(dd, dr))
        def _(dd=dd, dr=dr):
            hcopy(dd, dr).start()

    def piece_sent(c, carry):
        @pl.when(c != d)
        def _():
            pcopy(c, d).wait_send()

        return carry

    lax.fori_loop(0, chunks, piece_sent, 0)
    for dd, dr in around:

        @pl.when(present(dd, dr))
        def _(dd=dd, dr=dr):
            hcopy(-dd, -dr).wait_recv()

    for dd, dr in around:

        @pl.when(present(dd, dr))
        def _(dd=dd, dr=dr):
            hcopy(dd, dr).wait_send()


def finish(depth_count, row_count, picture, side, settled_d, settled_v, filtered, out_d, out_v, sem):
    zn = settled_d.shape[0]
    part = zn // PARTS
    copies = []
    for p in range(PARTS):
        z = pl.ds(p * part, part)
        copies.append(pltpu.make_async_copy(settled_d.at[z], out_d.at[z], sem.at[0, p]))
        for k in range(3):
            copies.append(
                pltpu.make_async_copy(settled_v.at[k, z], out_v.at[k, z], sem.at[1 + k, p])
            )
    for copy in copies:
        copy.start()
    yn = filtered.shape[1]
    tiles = yn // SUB
    d = lax.axis_index("depth")
    r = lax.axis_index("row")
    lane = lax.broadcasted_iota(jnp.int32, (SUB, LANES), 1)
    sublane = lax.broadcasted_iota(jnp.int32, (SUB, LANES), 0)
    zero = jnp.zeros((SUB, LANES), jnp.float32)
    for t in range(tiles):
        own = [picture[i, pl.ds(SUB + t * SUB, SUB), :] for i in range(4)]
        centre = (own[0] + own[1] + own[2]) * (1.0 / 3.0)
        top = [zero] * 4
        bottom = zero
        for dy in range(-2, 3):
            rows = pl.ds(SUB + t * SUB + dy, SUB)
            y = sublane + (r * yn + t * SUB + dy)
            y_ok = (y >= 0) & (y < yn * row_count)
            mid = [picture[i, rows, :] for i in range(4)]
            before = [pltpu.roll(side[0, rows, :], LANES - 2 - 2 * i, 1) for i in range(4)]
            after = [pltpu.roll(side[1, rows, :], (LANES - 2 * i) % LANES, 1) for i in range(4)]
            for dx in range(-2, 3):
                x = lane + (d * LANES + dx)
                ok = y_ok & (x >= 0) & (x < LANES * depth_count)
                if dx < 0:
                    pixel = [
                        pltpu.roll(jnp.where(lane >= LANES + dx, before[i], mid[i]), -dx, 1)
                        for i in range(4)
                    ]
                elif dx > 0:
                    pixel = [
                        pltpu.roll(jnp.where(lane < dx, after[i], mid[i]), LANES - dx, 1)
                        for i in range(4)
                    ]
                else:
                    pixel = mid
                pixel = [jnp.where(ok, p, 0.0) for p in pixel]
                space = math.exp(-(dx * dx + dy * dy) / (2.0 * SPACE_SCALE * SPACE_SCALE))
                diff = (pixel[0] + pixel[1] + pixel[2]) * (1.0 / 3.0) - centre
                close = jnp.exp(diff * diff * (-1.0 / (2.0 * RANGE_SCALE * RANGE_SCALE)))
                weight = jnp.where(ok, space * close, 0.0)
                top = [top[i] + weight * pixel[i] for i in range(4)]
                bottom = bottom + weight
        for i in range(4):
            filtered[i, pl.ds(t * SUB, SUB), :] = top[i] / bottom
    for copy in copies:
        copy.wait()


def body(depth_count, row_count, density, velocity, palette):
    zn, yn, xn = density.shape
    chunks = xn // LANES
    assert chunks == depth_count and yn % SUB == 0
    f32 = jnp.float32
    dma = pltpu.SemaphoreType.DMA
    vmem = pltpu.VMEM
    hbm = pl.BlockSpec(memory_space=pltpu.HBM)
    on_chip = pl.BlockSpec(memory_space=vmem)
    picture, side, settled_d, settled_v = pl.pallas_call(
        functools.partial(kernel, depth_count, row_count),
        out_shape=(
            jax.ShapeDtypeStruct((4, yn + 2 * SUB, LANES), f32),
            jax.ShapeDtypeStruct((2, yn + 2 * SUB, LANES), f32),
            jax.ShapeDtypeStruct(density.shape, f32),
            jax.ShapeDtypeStruct(velocity.shape, f32),
        ),
        in_specs=[hbm, hbm, hbm],
        out_specs=(on_chip,) * 4,
        scratch_shapes=[
            vmem((4, zn + 4, chunks + 2, yn + 2 * SUB, LANES), f32),
            vmem((4, zn + 2, chunks + 2, yn + SUB, LANES), f32),
            vmem((4, 1, 1, xn), f32),
            vmem((4, 3, 1, 1, xn), f32),
            vmem((chunks, 4, yn, LANES), f32),
            vmem((chunks, 4, yn, LANES), f32),
            vmem((depth_count, 4, yn, LANES), f32),
            vmem((2, yn + 2 * SUB, LANES), f32),
            pltpu.SMEM((3, 4), f32),
            dma((2, chunks)),
            dma,
            dma((2, 2, chunks)),
            dma((2, 2, chunks)),
            dma((2, 2, chunks)),
            dma((2, 2, chunks)),
            dma((2, 4)),
            dma((2, 4)),
            dma((chunks,)),
            dma((depth_count,)),
            dma((8,)),
            dma((8,)),
        ],
        compiler_params=pltpu.CompilerParams(
            collective_id=0, has_side_effects=True, vmem_limit_bytes=48 * 2**20
        ),
        name="rheology",
    )(*(pltpu.with_memory_space_constraint(v, pltpu.HBM) for v in (density, velocity, palette)))
    return pl.pallas_call(
        functools.partial(finish, depth_count, row_count),
        out_shape=(
            jax.ShapeDtypeStruct((4, yn, LANES), f32),
            jax.ShapeDtypeStruct(density.shape, f32),
            jax.ShapeDtypeStruct(velocity.shape, f32),
        ),
        in_specs=[on_chip] * 4,
        out_specs=(on_chip, hbm, hbm),
        scratch_shapes=[dma((4, PARTS))],
        compiler_params=pltpu.CompilerParams(vmem_limit_bytes=8 * 2**20),
        name="finish",
    )(picture, side, settled_d, settled_v)


def solution(mesh):
    in_specs = (P("depth", "row", None), P(None, "depth", "row", None), P())
    out_specs = (P(None, "row", "depth"), P("depth", "row", None), P(None, "depth", "row", None))
    run = functools.partial(body, mesh.shape["depth"], mesh.shape["row"])
    return jax.shard_map(run, mesh=mesh, in_specs=in_specs, out_specs=out_specs, check_vma=False)
```

```python
import functools
import math

import jax
import jax.numpy as jnp
from jax import lax
from jax.experimental import pallas as pl
from jax.experimental.pallas import tpu as pltpu
from jax.sharding import PartitionSpec as P

DIFFUSION = 0.1
ADVECTION = 0.25
VISCOSITY = 0.15
FRICTION = 0.2
OPTICAL = 2.0
RANGE_SCALE = 0.1
SPACE_SCALE = 1.5
MESH = pl.DeviceIdType.MESH
LANES = 128
SUB = 8
PARTS = 2
FAR = 1.0e6


def shifted_pair(before, here, after, first, last):
    left = pltpu.roll(jnp.where(last, before, here), 1, 1)
    right = pltpu.roll(jnp.where(first, after, here), LANES - 1, 1)
    return left, right


def divisor(n, most):
    return max([k for k in range(1, most + 1) if n and n % k == 0], default=1)


def step_tile(ref, z, block, row, first, last):
    def get(k, dz=0, dy=0, dx=0):
        return ref[k, z + dz, block + dx, pl.ds(row + dy, SUB), :]

    here = [get(k) for k in range(4)]
    sides = [
        shifted_pair(get(k, dx=-1), here[k], get(k, dx=1), first, last) for k in range(4)
    ]
    up = [get(k, dy=-1) for k in range(4)]
    down = [get(k, dy=1) for k in range(4)]
    front = [get(k, dz=-1) for k in range(4)]
    back = [get(k, dz=1) for k in range(4)]
    left = [s[0] for s in sides]
    right = [s[1] for s in sides]
    sums = [
        (left[k] + right[k]) + (up[k] + down[k]) + (front[k] + back[k]) for k in range(4)
    ]
    flux = (
        (right[0] * right[1] - left[0] * left[1])
        + (down[0] * down[2] - up[0] * up[2])
        + (back[0] * back[3] - front[0] * front[3])
    )
    r = here[0]
    squared = r * r
    new_r = (1.0 - 6.0 * DIFFUSION) * r + DIFFUSION * sums[0] - (0.5 * ADVECTION) * flux
    one = 1.0 + squared
    drag = 1.0 + FRICTION * squared
    inverse = 1.0 / (one * drag)
    side_w = VISCOSITY * squared * inverse
    own_w = one * inverse - 6.0 * side_w
    return [new_r] + [own_w * here[k] + side_w * sums[k] for k in range(1, 4)]


def kernel(
    depth_count,
    row_count,
    dens,
    vel,
    pal_hbm,
    mid,
    side,
    out_d,
    out_v,
    q0,
    q1,
    corner_d,
    corner_v,
    piece,
    pieces,
    edge,
    pal,
    load_sem,
    pal_sem,
    zsend,
    zrecv,
    rsend,
    rrecv,
    csend,
    crecv,
    word,
    psend,
    precv,
    hsend,
    hrecv,
):
    zn, yn = dens.shape[0], dens.shape[1]
    chunks = dens.shape[2] // LANES
    tiles = yn // SUB
    d = lax.axis_index("depth")
    r = lax.axis_index("row")
    has = {-1: (d > 0, r > 0), 1: (d < depth_count - 1, r < row_count - 1)}

    def present(dd, dr):
        ok = None
        for step, which in ((dd, 0), (dr, 1)):
            if step:
                ok = has[step][which] if ok is None else ok & has[step][which]
        return ok

    def where_is(dd, dr):
        return {"depth": d + dd, "row": r + dr}

    diagonal = [(dd, dr) for dd in (-1, 1) for dr in (-1, 1)]
    around = diagonal + [(-1, 0), (1, 0), (0, -1), (0, 1)]

    ring = [{"depth": lax.rem(d + k, depth_count), "row": r} for k in (1, depth_count - 1)]
    barrier = pltpu.get_barrier_semaphore()
    count = jnp.int32(2)
    for place in ring:
        pl.semaphore_signal(barrier, inc=1, device_id=place, device_id_type=MESH)
    for dr in (-1, 1):
        ok = has[dr][1]
        count = count + ok.astype(jnp.int32)

        @pl.when(ok)
        def _(dr=dr):
            pl.semaphore_signal(barrier, inc=1, device_id=where_is(0, dr), device_id_type=MESH)

    words = depth_count // 2 - 1

    def pass_word(k):
        for place in ring:
            pl.semaphore_signal(word.at[k], inc=1, device_id=place, device_id_type=MESH)

    def hear_word(k):
        pl.semaphore_wait(word.at[k], 2)

    def cols(c):
        return pl.ds(pl.multiple_of(c * LANES, LANES), LANES)

    def loads(c):
        rows = pl.ds(SUB, yn)
        return (
            pltpu.make_async_copy(
                dens.at[:, :, cols(c)], q0.at[0, pl.ds(2, zn), 1 + c, rows, :], load_sem.at[0, c]
            ),
            pltpu.make_async_copy(
                vel.at[:, :, :, cols(c)],
                q0.at[pl.ds(1, 3), pl.ds(2, zn), 1 + c, rows, :],
                load_sem.at[1, c],
            ),
        )

    def zcopies(c, dd):
        src = pl.ds(0, 2) if dd < 0 else pl.ds(zn - 2, 2)
        dst = pl.ds(zn + 2, 2) if dd < 0 else pl.ds(0, 2)
        side = (dd + 1) // 2
        rows = pl.ds(SUB, yn)
        return (
            pltpu.make_async_remote_copy(
                dens.at[src, :, cols(c)],
                q0.at[0, dst, 1 + c, rows, :],
                zsend.at[side, 0, c],
                zrecv.at[side, 0, c],
                device_id=where_is(dd, 0),
                device_id_type=MESH,
            ),
            pltpu.make_async_remote_copy(
                vel.at[:, src, :, cols(c)],
                q0.at[pl.ds(1, 3), dst, 1 + c, rows, :],
                zsend.at[side, 1, c],
                zrecv.at[side, 1, c],
                device_id=where_is(dd, 0),
                device_id_type=MESH,
            ),
        )

    def rcopies(c, dr):
        src = pl.ds(0, 2) if dr < 0 else pl.ds(yn - 2, 2)
        dst = pl.ds(SUB + yn, 2) if dr < 0 else pl.ds(SUB - 2, 2)
        side = (dr + 1) // 2
        return (
            pltpu.make_async_remote_copy(
                dens.at[:, src, cols(c)],
                q0.at[0, pl.ds(2, zn), 1 + c, dst, :],
                rsend.at[side, 0, c],
                rrecv.at[side, 0, c],
                device_id=where_is(0, dr),
                device_id_type=MESH,
            ),
            pltpu.make_async_remote_copy(
                vel.at[:, :, src, cols(c)],
                q0.at[pl.ds(1, 3), pl.ds(2, zn), 1 + c, dst, :],
                rsend.at[side, 1, c],
                rrecv.at[side, 1, c],
                device_id=where_is(0, dr),
                device_id_type=MESH,
            ),
        )

    def ccopies(dd, dr):
        z = pl.ds(0, 1) if dd < 0 else pl.ds(zn - 1, 1)
        y = pl.ds(0, 1) if dr < 0 else pl.ds(yn - 1, 1)
        slot = diagonal.index((-dd, -dr))
        return (
            pltpu.make_async_remote_copy(
                dens.at[z, y, :],
                corner_d.at[slot],
                csend.at[0, slot],
                crecv.at[0, slot],
                device_id=where_is(dd, dr),
                device_id_type=MESH,
            ),
            pltpu.make_async_remote_copy(
                vel.at[:, z, y, :],
                corner_v.at[slot],
                csend.at[1, slot],
                crecv.at[1, slot],
                device_id=where_is(dd, dr),
                device_id_type=MESH,
            ),
        )

    def start_loads(c, carry):
        for copy in loads(c):
            copy.start()
        return carry

    lax.fori_loop(0, chunks, start_loads, 0)
    pal_copy = pltpu.make_async_copy(pal_hbm, pal, pal_sem)
    pal_copy.start()
    pl.semaphore_wait(barrier, count)

    def start_layers(c, carry):
        for dd in (-1, 1):

            @pl.when(has[dd][0])
            def _(dd=dd):
                for copy in zcopies(c, dd):
                    copy.start()

        return carry

    def start_rows(c, carry):
        for dr in (-1, 1):

            @pl.when(has[dr][1])
            def _(dr=dr):
                for copy in rcopies(c, dr):
                    copy.start()

        return carry

    start_layers(0, 0)
    pass_word(0)
    start_layers(1, 0)
    lax.fori_loop(0, chunks, start_rows, 0)
    zero = jnp.zeros((SUB, LANES), jnp.float32)

    def pad_q0(z, carry):
        for k in range(4):
            for block in (0, chunks + 1):
                for t in range(tiles + 2):
                    q0[k, z, block, pl.ds(t * SUB, SUB), :] = zero
        return carry

    def pad_q1(z, carry):
        for k in range(4):
            for block in (0, chunks + 1):
                for t in range(tiles + 1):
                    q1[k, z, block, pl.ds(t * SUB, SUB), :] = zero
        return carry

    lax.fori_loop(1, zn + 3, pad_q0, 0)
    lax.fori_loop(0, zn + 2, pad_q1, 0)
    for dd in (-1, 1):
        layer = 1 if dd < 0 else zn + 2

        @pl.when(jnp.logical_not(has[dd][0]))
        def _(layer=layer):
            def clear(c, carry):
                for k in range(4):
                    for t in range(tiles + 2):
                        q0[k, layer, 1 + c, pl.ds(t * SUB, SUB), :] = zero
                return carry

            lax.fori_loop(0, chunks, clear, 0)

    for dr in (-1, 1):
        top = 0 if dr < 0 else SUB + yn

        @pl.when(jnp.logical_not(has[dr][1]))
        def _(top=top):
            def clear(z, carry):
                for k in range(4):
                    for c in range(chunks):
                        q0[k, z, 1 + c, pl.ds(top, SUB), :] = zero
                return carry

            lax.fori_loop(1, zn + 3, clear, 0)

    hear_word(0)
    if words > 1:
        pass_word(1)
    for dd, dr in diagonal:

        @pl.when(present(dd, dr))
        def _(dd=dd, dr=dr):
            for copy in ccopies(dd, dr):
                copy.start()

    lax.fori_loop(2, chunks, start_layers, 0)

    lane = lax.broadcasted_iota(jnp.int32, (SUB, LANES), 1)
    sublane = lax.broadcasted_iota(jnp.int32, (SUB, LANES), 0)
    first, last = lane == 0, lane == LANES - 1

    def wait_layers(c):
        for dd in (-1, 1):

            @pl.when(has[dd][0])
            def _(dd=dd):
                for copy in zcopies(c, -dd):
                    copy.wait_recv()

    def wait_own(c):
        for copy in loads(c):
            copy.wait()

    def wait_rows(c):
        for dr in (-1, 1):

            @pl.when(has[dr][1])
            def _(dr=dr):
                for copy in rcopies(c, -dr):
                    copy.wait_recv()

    low_row = jnp.where(r > 0, -1, 0)
    high_row = jnp.where(r < row_count - 1, yn, yn - 1)
    row_ok = []
    for t in range(tiles + 1):
        y = sublane + (t * SUB - 1)
        row_ok.append((y >= low_row) & (y <= high_row))
    low_z = jnp.where(d > 0, 0, 1)
    high_z = jnp.where(d < depth_count - 1, zn + 1, zn)

    def first_step(c, z, which, edge_layer):
        inside = (z >= low_z) & (z <= high_z) if edge_layer else None
        for t in which:
            new = step_tile(q0, z + 1, 1 + c, SUB - 1 + t * SUB, first, last)
            ok = row_ok[t] if t in (0, tiles) else None
            if edge_layer:
                ok = inside if ok is None else ok & inside
            for k in range(4):
                q1[k, z, 1 + c, pl.ds(t * SUB, SUB), :] = (
                    new[k] if ok is None else jnp.where(ok, new[k], 0.0)
                )

    def first_inner(c, which):
        def layer(z, carry):
            first_step(c, z, which, False)
            return carry

        lax.fori_loop(2, zn, layer, 0, unroll=divisor(zn - 2, 7))

    def first_outer(c):
        for z in (0, 1, zn, zn + 1):
            first_step(c, z, range(tiles + 1), z in (0, zn + 1))

    pal_copy.wait()
    weights = [[0.5 * pal[i, k] for k in range(4)] for i in range(3)]
    thickness = OPTICAL / (zn * depth_count)

    def second_step(c, z, carry):
        at = cols(c)
        out = []
        for t in range(tiles):
            through, *shades = carry[t]
            new = step_tile(q1, z + 1, 1 + c, 1 + t * SUB, first, last)
            rows = pl.ds(t * SUB, SUB)
            out_d[z, rows, at] = new[0]
            for k in range(3):
                out_v[k, z, rows, at] = new[1 + k]
            beyond = through * jnp.exp((-thickness) * new[0] * new[0])
            emitted = through - beyond
            lit = []
            for i in range(3):
                dot = weights[i][0] * new[0]
                for k in range(1, 4):
                    dot = dot + weights[i][k] * new[k]
                lit.append(shades[i] + emitted * jnp.tanh(dot))
            out.append((beyond, *lit))
        return tuple(out)

    clear_view = tuple((jnp.ones((SUB, LANES), jnp.float32), zero, zero, zero) for _ in range(tiles))

    def second(c):
        def layer(z, carry):
            return second_step(c, z, carry)

        done = lax.fori_loop(0, zn, layer, clear_view, unroll=divisor(zn, 8))
        for t in range(tiles):
            through, *shades = done[t]
            rows = pl.ds(t * SUB, SUB)
            for i in range(3):
                piece[c, i, rows, :] = 0.5 * ((1.0 - through) + shades[i])
            piece[c, 3, rows, :] = through

    def pcopy(c, source):
        return pltpu.make_async_remote_copy(
            piece.at[c],
            pieces.at[source],
            psend.at[c],
            precv.at[source],
            device_id={"depth": c, "row": r},
            device_id_type=MESH,
        )

    def hand_over(c):
        @pl.when(c != d)
        def _():
            pcopy(c, d).start()

        @pl.when(c == d)
        def _():
            pieces[d] = piece[c]

    wait_own(0)

    def innermost(i, carry):
        @pl.when(i + 1 < chunks)
        def _():
            wait_own(i + 1)

        first_inner(i, range(1, tiles))
        return carry

    lax.fori_loop(0, chunks, innermost, 0)
    if words > 1:
        hear_word(1)
    if words > 2:
        pass_word(2)

    for dd, dr in diagonal:

        @pl.when(present(dd, dr))
        def _(dd=dd, dr=dr):
            slot = diagonal.index((dd, dr))
            for copy in ccopies(-dd, -dr):
                copy.wait_recv()
            z = 1 if dd < 0 else zn + 2
            y = SUB - 1 if dr < 0 else SUB + yn
            for c in range(chunks):
                at = pl.ds(c * LANES, LANES)
                q0[0, z, 1 + c, pl.ds(y, 1), :] = corner_d[slot, 0, :, at]
                for k in range(3):
                    q0[1 + k, z, 1 + c, pl.ds(y, 1), :] = corner_v[slot, k, 0, :, at]

    wait_rows(0)
    wait_layers(0)

    def work(i, carry):
        @pl.when(i + 1 < chunks)
        def _():
            wait_rows(i + 1)
            wait_layers(i + 1)

        @pl.when(i == chunks - 2)
        def _():
            for c in range(2, chunks - 3):
                hand_over(c)

        @pl.when(i < chunks)
        def _():
            first_inner(i, (0, tiles))
            first_outer(i)

        for k in range(2, words):

            @pl.when(i == k - 1)
            def _(k=k):
                hear_word(k)
                if k + 1 < words:
                    pass_word(k + 1)

        @pl.when(i >= 1)
        def _():
            second(i - 1)
            pl.when((i <= 2) | (i >= chunks - 2))(lambda: hand_over(i - 1))

        return carry

    lax.fori_loop(0, chunks + 1, work, 0)

    def sent(c, carry):
        for dd in (-1, 1):

            @pl.when(has[dd][0])
            def _(dd=dd):
                for copy in zcopies(c, dd):
                    copy.wait_send()

        for dr in (-1, 1):

            @pl.when(has[dr][1])
            def _(dr=dr):
                for copy in rcopies(c, dr):
                    copy.wait_send()

        return carry

    lax.fori_loop(0, chunks, sent, 0)
    for dd, dr in diagonal:

        @pl.when(present(dd, dr))
        def _(dd=dd, dr=dr):
            for copy in ccopies(dd, dr):
                copy.wait_send()

    def wait_piece(k, carry):
        @pl.when(k != d)
        def _():
            pcopy(k, k).wait_recv()

        return carry

    lax.fori_loop(0, depth_count, wait_piece, 0)

    for t in range(tiles):
        rows = pl.ds(t * SUB, SUB)
        through = pieces[0, 3, rows, :]
        colour = [pieces[0, i, rows, :] for i in range(3)]
        for k in range(1, depth_count):
            for i in range(3):
                colour[i] = colour[i] + through * pieces[k, i, rows, :]
            through = through * pieces[k, 3, rows, :]
        pixel = colour + [1.0 - through]
        rows = pl.ds(SUB + t * SUB, SUB)
        left, right = pixel[0], pltpu.roll(pixel[0], 2, 1)
        for i in range(4):
            mid[i, rows, :] = pixel[i]
            if i:
                left = jnp.where(lane >= 2 * i, pltpu.roll(pixel[i], 2 * i, 1), left)
                right = jnp.where(lane >= 2 * i, pltpu.roll(pixel[i], 2 * i + 2, 1), right)
        edge[0, rows, :] = left
        edge[1, rows, :] = right

    def hcopy(dd, dr):
        if dr == 0:
            src = dst = pl.ds(SUB, yn)
        elif dr < 0:
            src, dst = pl.ds(SUB, 2), pl.ds(SUB + yn, 2)
        else:
            src, dst = pl.ds(SUB + yn - 2, 2), pl.ds(SUB - 2, 2)
        slot = around.index((-dd, -dr))
        if dd:
            ends = edge.at[(dd + 1) // 2, src, :], side.at[(1 - dd) // 2, dst, :]
        else:
            ends = mid.at[:, src, :], mid.at[:, dst, :]
        return pltpu.make_async_remote_copy(
            *ends,
            hsend.at[slot],
            hrecv.at[slot],
            device_id=where_is(dd, dr),
            device_id_type=MESH,
        )

    for dd, dr in around:

        @pl.when(present(dd, dr))
        def _(dd=dd, dr=dr):
            hcopy(dd, dr).start()

    def piece_sent(c, carry):
        @pl.when(c != d)
        def _():
            pcopy(c, d).wait_send()

        return carry

    lax.fori_loop(0, chunks, piece_sent, 0)
    for dd, dr in around:

        @pl.when(present(dd, dr))
        def _(dd=dd, dr=dr):
            hcopy(-dd, -dr).wait_recv()

    for dd, dr in around:

        @pl.when(present(dd, dr))
        def _(dd=dd, dr=dr):
            hcopy(dd, dr).wait_send()


def finish(depth_count, row_count, picture, side, settled_d, settled_v, filtered, out_d, out_v, moved, sem):
    zn = settled_d.shape[0]
    part = zn // PARTS
    copies = []
    for p in range(PARTS):
        z = pl.ds(p * part, part)
        copies.append(pltpu.make_async_copy(settled_d.at[z], out_d.at[z], sem.at[0, p]))
        for k in range(3):
            copies.append(
                pltpu.make_async_copy(settled_v.at[k, z], out_v.at[k, z], sem.at[1 + k, p])
            )
    for copy in copies:
        copy.start()
    yn = filtered.shape[1]
    tiles = yn // SUB
    d = lax.axis_index("depth")
    r = lax.axis_index("row")
    lane = lax.broadcasted_iota(jnp.int32, (SUB, LANES), 1)
    sublane = lax.broadcasted_iota(jnp.int32, (SUB, LANES), 0)
    zero = jnp.zeros((SUB, LANES), jnp.float32)
    for t in range(tiles + 2):
        rows = pl.ds(t * SUB, SUB)
        y = sublane + (r * yn + (t - 1) * SUB)
        y_ok = (y >= 0) & (y < yn * row_count)
        own = [picture[i, rows, :] for i in range(4)]
        low, high = side[0, rows, :], side[1, rows, :]
        before = [
            jnp.where(lane >= LANES - 2, pltpu.roll(low, LANES - 2 - 2 * i, 1), own[i])
            for i in range(4)
        ]
        after = [
            jnp.where(lane < 2, pltpu.roll(high, LANES - 2 * i, 1) if i else high, own[i])
            for i in range(4)
        ]
        for dx in range(-2, 3):
            x = lane + (d * LANES + dx)
            ok = y_ok & (x >= 0) & (x < LANES * depth_count)
            if dx < 0:
                pixel = [
                    pltpu.roll(jnp.where(lane >= LANES + dx, before[i], own[i]), -dx, 1)
                    for i in range(4)
                ]
            elif dx > 0:
                pixel = [
                    pltpu.roll(jnp.where(lane < dx, after[i], own[i]), LANES - dx, 1)
                    for i in range(4)
                ]
            else:
                pixel = own
            pixel = [jnp.where(ok, p, 0.0) for p in pixel]
            for i in range(4):
                moved[dx + 2, i, rows, :] = pixel[i]
            moved[dx + 2, 4, rows, :] = jnp.where(
                ok, (pixel[0] + pixel[1] + pixel[2]) * (1.0 / 3.0), FAR
            )
    for t in range(tiles):
        centre = moved[2, 4, pl.ds(SUB + t * SUB, SUB), :]
        top = [zero] * 4
        bottom = zero
        for dy in range(-2, 3):
            rows = pl.ds(SUB + t * SUB + dy, SUB)
            for dx in range(-2, 3):
                space = math.exp(-(dx * dx + dy * dy) / (2.0 * SPACE_SCALE * SPACE_SCALE))
                diff = moved[dx + 2, 4, rows, :] - centre
                close = jnp.exp(diff * diff * (-1.0 / (2.0 * RANGE_SCALE * RANGE_SCALE)))
                weight = space * close
                top = [top[i] + weight * moved[dx + 2, i, rows, :] for i in range(4)]
                bottom = bottom + weight
        inverse = 1.0 / bottom
        for i in range(4):
            filtered[i, pl.ds(t * SUB, SUB), :] = top[i] * inverse

    for copy in copies:
        copy.wait()


def body(depth_count, row_count, density, velocity, palette):
    zn, yn, xn = density.shape
    chunks = xn // LANES
    assert chunks == depth_count and yn % SUB == 0
    f32 = jnp.float32
    dma = pltpu.SemaphoreType.DMA
    vmem = pltpu.VMEM
    hbm = pl.BlockSpec(memory_space=pltpu.HBM)
    on_chip = pl.BlockSpec(memory_space=vmem)
    picture, side, settled_d, settled_v = pl.pallas_call(
        functools.partial(kernel, depth_count, row_count),
        out_shape=(
            jax.ShapeDtypeStruct((4, yn + 2 * SUB, LANES), f32),
            jax.ShapeDtypeStruct((2, yn + 2 * SUB, LANES), f32),
            jax.ShapeDtypeStruct(density.shape, f32),
            jax.ShapeDtypeStruct(velocity.shape, f32),
        ),
        in_specs=[hbm, hbm, hbm],
        out_specs=(on_chip,) * 4,
        scratch_shapes=[
            vmem((4, zn + 4, chunks + 2, yn + 2 * SUB, LANES), f32),
            vmem((4, zn + 2, chunks + 2, yn + SUB, LANES), f32),
            vmem((4, 1, 1, xn), f32),
            vmem((4, 3, 1, 1, xn), f32),
            vmem((chunks, 4, yn, LANES), f32),
            vmem((depth_count, 4, yn, LANES), f32),
            vmem((2, yn + 2 * SUB, LANES), f32),
            pltpu.SMEM((3, 4), f32),
            dma((2, chunks)),
            dma,
            dma((2, 2, chunks)),
            dma((2, 2, chunks)),
            dma((2, 2, chunks)),
            dma((2, 2, chunks)),
            dma((2, 4)),
            dma((2, 4)),
            pltpu.SemaphoreType.REGULAR((max(1, depth_count // 2 - 1),)),
            dma((chunks,)),
            dma((depth_count,)),
            dma((8,)),
            dma((8,)),
        ],
        compiler_params=pltpu.CompilerParams(
            collective_id=0, has_side_effects=True, vmem_limit_bytes=48 * 2**20
        ),
        name="rheology",
    )(*(pltpu.with_memory_space_constraint(v, pltpu.HBM) for v in (density, velocity, palette)))
    return pl.pallas_call(
        functools.partial(finish, depth_count, row_count),
        out_shape=(
            jax.ShapeDtypeStruct((4, yn, LANES), f32),
            jax.ShapeDtypeStruct(density.shape, f32),
            jax.ShapeDtypeStruct(velocity.shape, f32),
        ),
        in_specs=[on_chip] * 4,
        out_specs=(on_chip, hbm, hbm),
        scratch_shapes=[vmem((5, 5, yn + 2 * SUB, LANES), f32), dma((4, PARTS))],
        compiler_params=pltpu.CompilerParams(vmem_limit_bytes=8 * 2**20),
        name="finish",
    )(picture, side, settled_d, settled_v)


def solution(mesh):
    in_specs = (P("depth", "row", None), P(None, "depth", "row", None), P())
    out_specs = (P(None, "row", "depth"), P("depth", "row", None), P(None, "depth", "row", None))
    run = functools.partial(body, mesh.shape["depth"], mesh.shape["row"])
    return jax.shard_map(run, mesh=mesh, in_specs=in_specs, out_specs=out_specs, check_vma=False)
```

```python
import functools
import math

import jax
import jax.numpy as jnp
from jax import lax
from jax.experimental import pallas as pl
from jax.experimental.pallas import tpu as pltpu
from jax.sharding import PartitionSpec as P

DIFFUSION = 0.1
ADVECTION = 0.25
VISCOSITY = 0.15
FRICTION = 0.2
OPTICAL = 2.0
RANGE_SCALE = 0.1
SPACE_SCALE = 1.5
MESH = pl.DeviceIdType.MESH
LANES = 128
SUB = 8
PARTS = 1
FAR = 1.0e6


def shifted_pair(before, here, after, first, last):
    left = pltpu.roll(jnp.where(last, before, here), 1, 1)
    right = pltpu.roll(jnp.where(first, after, here), LANES - 1, 1)
    return left, right


def divisor(n, most):
    return max([k for k in range(1, most + 1) if n and n % k == 0], default=1)


def step_tile(ref, z, block, row, first, last):
    def get(k, dz=0, dy=0, dx=0):
        return ref[k, z + dz, block + dx, pl.ds(row + dy, SUB), :]

    here = [get(k) for k in range(4)]
    sides = [
        shifted_pair(get(k, dx=-1), here[k], get(k, dx=1), first, last) for k in range(4)
    ]
    up = [get(k, dy=-1) for k in range(4)]
    down = [get(k, dy=1) for k in range(4)]
    front = [get(k, dz=-1) for k in range(4)]
    back = [get(k, dz=1) for k in range(4)]
    left = [s[0] for s in sides]
    right = [s[1] for s in sides]
    sums = [
        (left[k] + right[k]) + (up[k] + down[k]) + (front[k] + back[k]) for k in range(4)
    ]
    flux = (
        (right[0] * right[1] - left[0] * left[1])
        + (down[0] * down[2] - up[0] * up[2])
        + (back[0] * back[3] - front[0] * front[3])
    )
    r = here[0]
    squared = r * r
    new_r = (1.0 - 6.0 * DIFFUSION) * r + DIFFUSION * sums[0] - (0.5 * ADVECTION) * flux
    one = 1.0 + squared
    drag = 1.0 + FRICTION * squared
    inverse = 1.0 / (one * drag)
    side_w = VISCOSITY * squared * inverse
    own_w = one * inverse - 6.0 * side_w
    return [new_r] + [own_w * here[k] + side_w * sums[k] for k in range(1, 4)]


def kernel(
    depth_count,
    row_count,
    dens,
    vel,
    pal_hbm,
    mid,
    side,
    out_d,
    out_v,
    q0,
    q1,
    corner_d,
    corner_v,
    piece,
    pieces,
    edge,
    pal,
    load_sem,
    pal_sem,
    zsend,
    zrecv,
    rsend,
    rrecv,
    csend,
    crecv,
    word,
    psend,
    precv,
    hsend,
    hrecv,
):
    zn, yn = dens.shape[0], dens.shape[1]
    chunks = dens.shape[2] // LANES
    tiles = yn // SUB
    d = lax.axis_index("depth")
    r = lax.axis_index("row")
    has = {-1: (d > 0, r > 0), 1: (d < depth_count - 1, r < row_count - 1)}

    def present(dd, dr):
        ok = None
        for step, which in ((dd, 0), (dr, 1)):
            if step:
                ok = has[step][which] if ok is None else ok & has[step][which]
        return ok

    def where_is(dd, dr):
        return {"depth": d + dd, "row": r + dr}

    diagonal = [(dd, dr) for dd in (-1, 1) for dr in (-1, 1)]
    around = diagonal + [(-1, 0), (1, 0), (0, -1), (0, 1)]

    ring = [{"depth": lax.rem(d + k, depth_count), "row": r} for k in (1, depth_count - 1)]
    barrier = pltpu.get_barrier_semaphore()
    count = jnp.int32(2)
    for place in ring:
        pl.semaphore_signal(barrier, inc=1, device_id=place, device_id_type=MESH)
    for dr in (-1, 1):
        ok = has[dr][1]
        count = count + ok.astype(jnp.int32)

        @pl.when(ok)
        def _(dr=dr):
            pl.semaphore_signal(barrier, inc=1, device_id=where_is(0, dr), device_id_type=MESH)

    words = depth_count // 2 - 1

    def pass_word(k):
        for place in ring:
            pl.semaphore_signal(word.at[k], inc=1, device_id=place, device_id_type=MESH)

    def hear_word(k):
        pl.semaphore_wait(word.at[k], 2)

    def cols(c):
        return pl.ds(pl.multiple_of(c * LANES, LANES), LANES)

    def loads(c):
        rows = pl.ds(SUB, yn)
        return (
            pltpu.make_async_copy(
                dens.at[:, :, cols(c)], q0.at[0, pl.ds(2, zn), 1 + c, rows, :], load_sem.at[0, c]
            ),
            pltpu.make_async_copy(
                vel.at[:, :, :, cols(c)],
                q0.at[pl.ds(1, 3), pl.ds(2, zn), 1 + c, rows, :],
                load_sem.at[1, c],
            ),
        )

    def zcopies(c, dd):
        src = pl.ds(0, 2) if dd < 0 else pl.ds(zn - 2, 2)
        dst = pl.ds(zn + 2, 2) if dd < 0 else pl.ds(0, 2)
        side = (dd + 1) // 2
        rows = pl.ds(SUB, yn)
        return (
            pltpu.make_async_remote_copy(
                dens.at[src, :, cols(c)],
                q0.at[0, dst, 1 + c, rows, :],
                zsend.at[side, 0, c],
                zrecv.at[side, 0, c],
                device_id=where_is(dd, 0),
                device_id_type=MESH,
            ),
            pltpu.make_async_remote_copy(
                vel.at[:, src, :, cols(c)],
                q0.at[pl.ds(1, 3), dst, 1 + c, rows, :],
                zsend.at[side, 1, c],
                zrecv.at[side, 1, c],
                device_id=where_is(dd, 0),
                device_id_type=MESH,
            ),
        )

    def rcopies(c, dr):
        src = pl.ds(0, 2) if dr < 0 else pl.ds(yn - 2, 2)
        dst = pl.ds(SUB + yn, 2) if dr < 0 else pl.ds(SUB - 2, 2)
        side = (dr + 1) // 2
        return (
            pltpu.make_async_remote_copy(
                dens.at[:, src, cols(c)],
                q0.at[0, pl.ds(2, zn), 1 + c, dst, :],
                rsend.at[side, 0, c],
                rrecv.at[side, 0, c],
                device_id=where_is(0, dr),
                device_id_type=MESH,
            ),
            pltpu.make_async_remote_copy(
                vel.at[:, :, src, cols(c)],
                q0.at[pl.ds(1, 3), pl.ds(2, zn), 1 + c, dst, :],
                rsend.at[side, 1, c],
                rrecv.at[side, 1, c],
                device_id=where_is(0, dr),
                device_id_type=MESH,
            ),
        )

    def ccopies(dd, dr):
        z = pl.ds(0, 1) if dd < 0 else pl.ds(zn - 1, 1)
        y = pl.ds(0, 1) if dr < 0 else pl.ds(yn - 1, 1)
        slot = diagonal.index((-dd, -dr))
        return (
            pltpu.make_async_remote_copy(
                dens.at[z, y, :],
                corner_d.at[slot],
                csend.at[0, slot],
                crecv.at[0, slot],
                device_id=where_is(dd, dr),
                device_id_type=MESH,
            ),
            pltpu.make_async_remote_copy(
                vel.at[:, z, y, :],
                corner_v.at[slot],
                csend.at[1, slot],
                crecv.at[1, slot],
                device_id=where_is(dd, dr),
                device_id_type=MESH,
            ),
        )

    def start_loads(c, carry):
        for copy in loads(c):
            copy.start()
        return carry

    lax.fori_loop(0, chunks, start_loads, 0)
    pal_copy = pltpu.make_async_copy(pal_hbm, pal, pal_sem)
    pal_copy.start()
    pl.semaphore_wait(barrier, count)

    def start_layers(c, carry):
        for dd in (-1, 1):

            @pl.when(has[dd][0])
            def _(dd=dd):
                for copy in zcopies(c, dd):
                    copy.start()

        return carry

    def start_rows(c, carry):
        for dr in (-1, 1):

            @pl.when(has[dr][1])
            def _(dr=dr):
                for copy in rcopies(c, dr):
                    copy.start()

        return carry

    start_layers(0, 0)
    pass_word(0)
    start_layers(1, 0)
    lax.fori_loop(0, chunks, start_rows, 0)
    zero = jnp.zeros((SUB, LANES), jnp.float32)

    def pad_q0(z, carry):
        for k in range(4):
            for block in (0, chunks + 1):
                for t in range(tiles + 2):
                    q0[k, z, block, pl.ds(t * SUB, SUB), :] = zero
        return carry

    def pad_q1(z, carry):
        for k in range(4):
            for block in (0, chunks + 1):
                for t in range(tiles + 1):
                    q1[k, z, block, pl.ds(t * SUB, SUB), :] = zero
        return carry

    lax.fori_loop(1, zn + 3, pad_q0, 0)
    lax.fori_loop(0, zn + 2, pad_q1, 0)
    for dd in (-1, 1):
        layer = 1 if dd < 0 else zn + 2

        @pl.when(jnp.logical_not(has[dd][0]))
        def _(layer=layer):
            def clear(c, carry):
                for k in range(4):
                    for t in range(tiles + 2):
                        q0[k, layer, 1 + c, pl.ds(t * SUB, SUB), :] = zero
                return carry

            lax.fori_loop(0, chunks, clear, 0)

    for dr in (-1, 1):
        top = 0 if dr < 0 else SUB + yn

        @pl.when(jnp.logical_not(has[dr][1]))
        def _(top=top):
            def clear(z, carry):
                for k in range(4):
                    for c in range(chunks):
                        q0[k, z, 1 + c, pl.ds(top, SUB), :] = zero
                return carry

            lax.fori_loop(1, zn + 3, clear, 0)

    hear_word(0)
    if words > 1:
        pass_word(1)
    for dd, dr in diagonal:

        @pl.when(present(dd, dr))
        def _(dd=dd, dr=dr):
            for copy in ccopies(dd, dr):
                copy.start()

    lax.fori_loop(2, chunks, start_layers, 0)

    lane = lax.broadcasted_iota(jnp.int32, (SUB, LANES), 1)
    sublane = lax.broadcasted_iota(jnp.int32, (SUB, LANES), 0)
    first, last = lane == 0, lane == LANES - 1

    def wait_layers(c):
        for dd in (-1, 1):

            @pl.when(has[dd][0])
            def _(dd=dd):
                for copy in zcopies(c, -dd):
                    copy.wait_recv()

    def wait_own(c):
        for copy in loads(c):
            copy.wait()

    def wait_rows(c):
        for dr in (-1, 1):

            @pl.when(has[dr][1])
            def _(dr=dr):
                for copy in rcopies(c, -dr):
                    copy.wait_recv()

    low_row = jnp.where(r > 0, -1, 0)
    high_row = jnp.where(r < row_count - 1, yn, yn - 1)
    row_ok = []
    for t in range(tiles + 1):
        y = sublane + (t * SUB - 1)
        row_ok.append((y >= low_row) & (y <= high_row))
    low_z = jnp.where(d > 0, 0, 1)
    high_z = jnp.where(d < depth_count - 1, zn + 1, zn)

    def first_step(c, z, which, edge_layer):
        inside = (z >= low_z) & (z <= high_z) if edge_layer else None
        for t in which:
            new = step_tile(q0, z + 1, 1 + c, SUB - 1 + t * SUB, first, last)
            ok = row_ok[t] if t in (0, tiles) else None
            if edge_layer:
                ok = inside if ok is None else ok & inside
            for k in range(4):
                q1[k, z, 1 + c, pl.ds(t * SUB, SUB), :] = (
                    new[k] if ok is None else jnp.where(ok, new[k], 0.0)
                )

    def first_inner(c, which):
        def layer(z, carry):
            first_step(c, z, which, False)
            return carry

        lax.fori_loop(2, zn, layer, 0, unroll=divisor(zn - 2, 7))

    def first_outer(c):
        for z in (0, 1, zn, zn + 1):
            first_step(c, z, range(tiles + 1), z in (0, zn + 1))

    pal_copy.wait()
    weights = [[0.5 * pal[i, k] for k in range(4)] for i in range(3)]
    thickness = OPTICAL / (zn * depth_count)

    def second_step(c, z, carry):
        at = cols(c)
        out = []
        for t in range(tiles):
            through, *shades = carry[t]
            new = step_tile(q1, z + 1, 1 + c, 1 + t * SUB, first, last)
            rows = pl.ds(t * SUB, SUB)
            out_d[z, rows, at] = new[0]
            for k in range(3):
                out_v[k, z, rows, at] = new[1 + k]
            beyond = through * jnp.exp((-thickness) * new[0] * new[0])
            emitted = through - beyond
            lit = []
            for i in range(3):
                dot = weights[i][0] * new[0]
                for k in range(1, 4):
                    dot = dot + weights[i][k] * new[k]
                lit.append(shades[i] + emitted * jnp.tanh(dot))
            out.append((beyond, *lit))
        return tuple(out)

    clear_view = tuple((jnp.ones((SUB, LANES), jnp.float32), zero, zero, zero) for _ in range(tiles))

    def second(c):
        def layer(z, carry):
            return second_step(c, z, carry)

        done = lax.fori_loop(0, zn, layer, clear_view, unroll=divisor(zn, 8))
        for t in range(tiles):
            through, *shades = done[t]
            rows = pl.ds(t * SUB, SUB)
            for i in range(3):
                piece[c, i, rows, :] = 0.5 * ((1.0 - through) + shades[i])
            piece[c, 3, rows, :] = through

    def pcopy(c, source):
        return pltpu.make_async_remote_copy(
            piece.at[c],
            pieces.at[source],
            psend.at[c],
            precv.at[source],
            device_id={"depth": c, "row": r},
            device_id_type=MESH,
        )

    def hand_over(c):
        @pl.when(c != d)
        def _():
            pcopy(c, d).start()

        @pl.when(c == d)
        def _():
            pieces[d] = piece[c]

    wait_own(0)

    def innermost(i, carry):
        @pl.when(i + 1 < chunks)
        def _():
            wait_own(i + 1)

        first_inner(i, range(1, tiles))
        return carry

    lax.fori_loop(0, chunks, innermost, 0)
    if words > 1:
        hear_word(1)
    if words > 2:
        pass_word(2)

    for dd, dr in diagonal:

        @pl.when(present(dd, dr))
        def _(dd=dd, dr=dr):
            slot = diagonal.index((dd, dr))
            for copy in ccopies(-dd, -dr):
                copy.wait_recv()
            z = 1 if dd < 0 else zn + 2
            y = SUB - 1 if dr < 0 else SUB + yn
            for c in range(chunks):
                at = pl.ds(c * LANES, LANES)
                q0[0, z, 1 + c, pl.ds(y, 1), :] = corner_d[slot, 0, :, at]
                for k in range(3):
                    q0[1 + k, z, 1 + c, pl.ds(y, 1), :] = corner_v[slot, k, 0, :, at]

    wait_rows(0)
    wait_layers(0)

    def work(i, carry):
        @pl.when(i + 1 < chunks)
        def _():
            wait_rows(i + 1)

        @pl.when(i < chunks)
        def _():
            first_inner(i, (0, tiles))

        @pl.when(i + 1 < chunks)
        def _():
            wait_layers(i + 1)

        @pl.when(i == chunks - 2)
        def _():
            for c in range(2, chunks - 3):
                hand_over(c)

        @pl.when(i < chunks)
        def _():
            first_outer(i)

        for k in range(2, words):

            @pl.when(i == k - 1)
            def _(k=k):
                hear_word(k)
                if k + 1 < words:
                    pass_word(k + 1)

        @pl.when(i >= 1)
        def _():
            second(i - 1)
            pl.when((i <= 2) | (i >= chunks - 2))(lambda: hand_over(i - 1))

        return carry

    lax.fori_loop(0, chunks + 1, work, 0)

    def sent(c, carry):
        for dd in (-1, 1):

            @pl.when(has[dd][0])
            def _(dd=dd):
                for copy in zcopies(c, dd):
                    copy.wait_send()

        for dr in (-1, 1):

            @pl.when(has[dr][1])
            def _(dr=dr):
                for copy in rcopies(c, dr):
                    copy.wait_send()

        return carry

    lax.fori_loop(0, chunks, sent, 0)
    for dd, dr in diagonal:

        @pl.when(present(dd, dr))
        def _(dd=dd, dr=dr):
            for copy in ccopies(dd, dr):
                copy.wait_send()

    seen = []
    for k in range(depth_count):

        @pl.when(k != d)
        def _(k=k):
            pcopy(k, k).wait_recv()

        for t in range(tiles):
            own = [pieces[k, i, pl.ds(t * SUB, SUB), :] for i in range(4)]
            if k == 0:
                seen.append(own)
            else:
                through = seen[t][3]
                seen[t] = [seen[t][i] + through * own[i] for i in range(3)] + [through * own[3]]
    for t in range(tiles):
        *colour, through = seen[t]
        pixel = colour + [1.0 - through]
        rows = pl.ds(SUB + t * SUB, SUB)
        left, right = pixel[0], pltpu.roll(pixel[0], 2, 1)
        for i in range(4):
            mid[i, rows, :] = pixel[i]
            if i:
                left = jnp.where(lane >= 2 * i, pltpu.roll(pixel[i], 2 * i, 1), left)
                right = jnp.where(lane >= 2 * i, pltpu.roll(pixel[i], 2 * i + 2, 1), right)
        edge[0, rows, :] = left
        edge[1, rows, :] = right

    def hcopy(dd, dr):
        if dr == 0:
            src = dst = pl.ds(SUB, yn)
        elif dr < 0:
            src, dst = pl.ds(SUB, 2), pl.ds(SUB + yn, 2)
        else:
            src, dst = pl.ds(SUB + yn - 2, 2), pl.ds(SUB - 2, 2)
        slot = around.index((-dd, -dr))
        if dd:
            ends = edge.at[(dd + 1) // 2, src, :], side.at[(1 - dd) // 2, dst, :]
        else:
            ends = mid.at[:, src, :], mid.at[:, dst, :]
        return pltpu.make_async_remote_copy(
            *ends,
            hsend.at[slot],
            hrecv.at[slot],
            device_id=where_is(dd, dr),
            device_id_type=MESH,
        )

    for dd, dr in around:

        @pl.when(present(dd, dr))
        def _(dd=dd, dr=dr):
            hcopy(dd, dr).start()

    def piece_sent(c, carry):
        @pl.when(c != d)
        def _():
            pcopy(c, d).wait_send()

        return carry

    lax.fori_loop(0, chunks, piece_sent, 0)
    for dd, dr in around:

        @pl.when(present(dd, dr))
        def _(dd=dd, dr=dr):
            hcopy(-dd, -dr).wait_recv()

    for dd, dr in around:

        @pl.when(present(dd, dr))
        def _(dd=dd, dr=dr):
            hcopy(dd, dr).wait_send()


def finish(depth_count, row_count, picture, side, settled_d, settled_v, filtered, out_d, out_v, moved, sem):
    zn = settled_d.shape[0]
    part = zn // PARTS
    copies = []
    for p in range(PARTS):
        z = pl.ds(p * part, part)
        copies.append(pltpu.make_async_copy(settled_d.at[z], out_d.at[z], sem.at[0, p]))
        for k in range(3):
            copies.append(
                pltpu.make_async_copy(settled_v.at[k, z], out_v.at[k, z], sem.at[1 + k, p])
            )
    for copy in copies:
        copy.start()
    yn = filtered.shape[1]
    tiles = yn // SUB
    d = lax.axis_index("depth")
    r = lax.axis_index("row")
    lane = lax.broadcasted_iota(jnp.int32, (SUB, LANES), 1)
    sublane = lax.broadcasted_iota(jnp.int32, (SUB, LANES), 0)
    zero = jnp.zeros((SUB, LANES), jnp.float32)
    for t in range(tiles + 2):
        rows = pl.ds(t * SUB, SUB)
        y = sublane + (r * yn + (t - 1) * SUB)
        y_ok = (y >= 0) & (y < yn * row_count)
        own = [picture[i, rows, :] for i in range(4)]
        low, high = side[0, rows, :], side[1, rows, :]
        before = [
            jnp.where(lane >= LANES - 2, pltpu.roll(low, LANES - 2 - 2 * i, 1), own[i])
            for i in range(4)
        ]
        after = [
            jnp.where(lane < 2, pltpu.roll(high, LANES - 2 * i, 1) if i else high, own[i])
            for i in range(4)
        ]
        for dx in range(-2, 3):
            x = lane + (d * LANES + dx)
            ok = y_ok & (x >= 0) & (x < LANES * depth_count)
            if dx < 0:
                pixel = [
                    pltpu.roll(jnp.where(lane >= LANES + dx, before[i], own[i]), -dx, 1)
                    for i in range(4)
                ]
            elif dx > 0:
                pixel = [
                    pltpu.roll(jnp.where(lane < dx, after[i], own[i]), LANES - dx, 1)
                    for i in range(4)
                ]
            else:
                pixel = own
            pixel = [jnp.where(ok, p, 0.0) for p in pixel]
            for i in range(4):
                moved[dx + 2, i, rows, :] = pixel[i]
            moved[dx + 2, 4, rows, :] = jnp.where(
                ok, (pixel[0] + pixel[1] + pixel[2]) * (1.0 / 3.0), FAR
            )
    for t in range(tiles):
        centre = moved[2, 4, pl.ds(SUB + t * SUB, SUB), :]
        top = [zero] * 4
        bottom = zero
        for dy in range(-2, 3):
            rows = pl.ds(SUB + t * SUB + dy, SUB)
            for dx in range(-2, 3):
                space = math.exp(-(dx * dx + dy * dy) / (2.0 * SPACE_SCALE * SPACE_SCALE))
                diff = moved[dx + 2, 4, rows, :] - centre
                close = jnp.exp(diff * diff * (-1.0 / (2.0 * RANGE_SCALE * RANGE_SCALE)))
                weight = space * close
                top = [top[i] + weight * moved[dx + 2, i, rows, :] for i in range(4)]
                bottom = bottom + weight
        inverse = 1.0 / bottom
        for i in range(4):
            filtered[i, pl.ds(t * SUB, SUB), :] = top[i] * inverse

    for copy in copies:
        copy.wait()


def body(depth_count, row_count, density, velocity, palette):
    zn, yn, xn = density.shape
    chunks = xn // LANES
    assert chunks == depth_count and yn % SUB == 0
    f32 = jnp.float32
    dma = pltpu.SemaphoreType.DMA
    vmem = pltpu.VMEM
    hbm = pl.BlockSpec(memory_space=pltpu.HBM)
    on_chip = pl.BlockSpec(memory_space=vmem)
    picture, side, settled_d, settled_v = pl.pallas_call(
        functools.partial(kernel, depth_count, row_count),
        out_shape=(
            jax.ShapeDtypeStruct((4, yn + 2 * SUB, LANES), f32),
            jax.ShapeDtypeStruct((2, yn + 2 * SUB, LANES), f32),
            jax.ShapeDtypeStruct(density.shape, f32),
            jax.ShapeDtypeStruct(velocity.shape, f32),
        ),
        in_specs=[hbm, hbm, hbm],
        out_specs=(on_chip,) * 4,
        scratch_shapes=[
            vmem((4, zn + 4, chunks + 2, yn + 2 * SUB, LANES), f32),
            vmem((4, zn + 2, chunks + 2, yn + SUB, LANES), f32),
            vmem((4, 1, 1, xn), f32),
            vmem((4, 3, 1, 1, xn), f32),
            vmem((chunks, 4, yn, LANES), f32),
            vmem((depth_count, 4, yn, LANES), f32),
            vmem((2, yn + 2 * SUB, LANES), f32),
            pltpu.SMEM((3, 4), f32),
            dma((2, chunks)),
            dma,
            dma((2, 2, chunks)),
            dma((2, 2, chunks)),
            dma((2, 2, chunks)),
            dma((2, 2, chunks)),
            dma((2, 4)),
            dma((2, 4)),
            pltpu.SemaphoreType.REGULAR((max(1, depth_count // 2 - 1),)),
            dma((chunks,)),
            dma((depth_count,)),
            dma((8,)),
            dma((8,)),
        ],
        compiler_params=pltpu.CompilerParams(
            collective_id=0, has_side_effects=True, vmem_limit_bytes=48 * 2**20
        ),
        name="rheology",
    )(*(pltpu.with_memory_space_constraint(v, pltpu.HBM) for v in (density, velocity, palette)))
    return pl.pallas_call(
        functools.partial(finish, depth_count, row_count),
        out_shape=(
            jax.ShapeDtypeStruct((4, yn, LANES), f32),
            jax.ShapeDtypeStruct(density.shape, f32),
            jax.ShapeDtypeStruct(velocity.shape, f32),
        ),
        in_specs=[on_chip] * 4,
        out_specs=(on_chip, hbm, hbm),
        scratch_shapes=[vmem((5, 5, yn + 2 * SUB, LANES), f32), dma((4, PARTS))],
        compiler_params=pltpu.CompilerParams(vmem_limit_bytes=8 * 2**20),
        name="finish",
    )(picture, side, settled_d, settled_v)


def solution(mesh):
    in_specs = (P("depth", "row", None), P(None, "depth", "row", None), P())
    out_specs = (P(None, "row", "depth"), P("depth", "row", None), P(None, "depth", "row", None))
    run = functools.partial(body, mesh.shape["depth"], mesh.shape["row"])
    return jax.shard_map(run, mesh=mesh, in_specs=in_specs, out_specs=out_specs, check_vma=False)
```
